32 devices in a mesh: day: 2 (over y), stu: 16 (over z, x, core).
Axes of the slice: x: 2, y: 2, z: 4, core: 2. Of those that a mesh axis runs over, the one named last changes fastest.
Arguments:
- performance: bfloat16 [64, 128, 1024], P('day', 'stu'), may hold values from -8 to 8
- student_factor: bfloat16 [128, 256], P('stu'), may hold values from -0.5 to 0.5
- skill_factor: bfloat16 [1024, 256], replicated, may hold values from -0.1875 to 0.1875
- day_prev: float32 [64, 256], P('day'), may hold values from -6 to 6
- ar_coef: float32 [7], replicated, may hold values from -0.3 to 0.3
Outputs:
- day_factor: float32 [64, 256], P('day', 'stu')
- residual: float32 [64, 256], P('day', 'stu')
The draws below stay inside these ranges and needn't reach their ends.
All inputs are finite; a program needn't handle non-finite values.
Results may differ from the reference program's by a relative error of at most 0.0003.
Values sent between devices are 32-bit elements; how exact they have to be, the bound alone decides.
No kernel may reach another device: no remote copies, remote signals or barrier semaphores. Data moves between devices by JAX's collectives and lax.ppermute only.
A program may use at most 64 MiB of HBM per device.

```python
import jax
import jax.numpy as jnp
from jax import lax

RANK = 256
SKILLS = 1024
LAGS = 7
ITERS = 3
STUDENTS = 128
WINDOW = 64


def draw_performance(key, part):
    shape = (WINDOW, STUDENTS, SKILLS)
    day_scale = 0.5 + 1.5 * jnp.arange(WINDOW, dtype=jnp.float32) / (WINDOW - 1)
    values = jnp.clip(jax.random.normal(key, shape, jnp.float32), -4.0, 4.0)
    return (values * day_scale[:, None, None]).astype(jnp.bfloat16)


def shard_levels(rng, extent, split, low, top_value):
    level, own = 1.0, jax.random.fold_in(rng, 6)
    for position, shards_of in split:
        heights = jnp.exp(jax.random.uniform(jax.random.fold_in(own, position), (shards_of,), jnp.float32, low / len(split), top_value / len(split)))
        level = level * jnp.repeat(heights, extent[position] // shards_of).reshape([-1 if axis == position else 1 for axis in range(len(extent))])
    return level


def bell_draw(key, shape, spread, limit, cuts=(), held_as=jnp.bfloat16):
    array = jax.random.normal(key, shape, jnp.float32) * spread
    if len(cuts) > 0:
        array = shard_levels(key, shape, cuts, -0.22, 0.18) * array
    return jnp.clip(array, min=-limit, max=limit).astype(held_as)


def setup_inputs(seed: int = 0) -> dict:
    key_of = jax.random.split(jax.random.key(seed), 6)
    return {
        "performance": draw_performance(jax.random.fold_in(key_of[5], 71), 0),
        "student_factor": bell_draw(key_of[1], (STUDENTS, RANK), STUDENTS ** -0.5, 0.5, ((0, 16),)),
        "skill_factor": bell_draw(key_of[2], (SKILLS, RANK), SKILLS ** -0.5, 0.1875),
        "day_prev": bell_draw(key_of[3], (WINDOW, RANK), 1.0, 6.0, ((0, 2),), jnp.float32),
        "ar_coef": jnp.clip(jax.random.uniform(key_of[4], (LAGS,), jnp.float32, -0.3, 0.3), -0.3, 0.3),
    }


smoothing = 1.0


def filter_ahead(values, coef):
    width = values.shape[0]
    padded = jnp.pad(values, ((LAGS, 0), (0, 0)))
    out = values
    for lag in range(1, LAGS + 1):
        out = out - coef[lag - 1] * padded[LAGS - lag:LAGS - lag + width]
    return out


def filter_back(values, coef):
    width = values.shape[0]
    padded = jnp.pad(values, ((0, LAGS), (0, 0)))
    out = values
    for lag in range(1, LAGS + 1):
        out = out - coef[lag - 1] * padded[lag:lag + width]
    return out


def operate(values, gram, coef):
    mixed = jnp.dot(values, gram, precision=lax.Precision.HIGHEST, preferred_element_type=jnp.float32)
    return mixed + smoothing * filter_back(filter_ahead(values, coef), coef)


def reference(performance, student_factor, skill_factor, day_prev, ar_coef):
    student_wide = student_factor.astype(jnp.float32)

    def one_day(slab):
        proj = jnp.dot(slab, skill_factor, preferred_element_type=jnp.float32)
        return jnp.sum(student_wide * proj, axis=0)

    mttkrp = lax.map(one_day, performance)
    gram = jnp.dot(student_factor.T, student_factor, preferred_element_type=jnp.float32) * jnp.dot(skill_factor.T, skill_factor, preferred_element_type=jnp.float32)
    day_factor = day_prev
    residual = mttkrp - operate(day_prev, gram, ar_coef)
    direction = residual
    norm_now = jnp.sum(residual * residual)
    for step in range(ITERS):
        image = operate(direction, gram, ar_coef)
        alpha = norm_now / jnp.sum(direction * image)
        day_factor = day_factor + alpha * direction
        residual = residual - alpha * image
        norm_next = jnp.sum(residual * residual)
        direction = residual + (norm_next / norm_now) * direction
        norm_now = norm_next
    return day_factor, residual
```

```python
import functools

import jax
import jax.numpy as jnp
from jax import lax
from jax.experimental import pallas as pl
from jax.experimental.pallas import tpu as pltpu
from jax.sharding import PartitionSpec as P

LAGS = 7
ITERS = 3
PAD = 8
LANES = 128
CHUNKS = 4


smoothing = 1.0


def exchange(block, axis, bit):
    route = [(i, i ^ bit) for i in range(lax.axis_size(axis))]
    return lax.ppermute(block, axis, route)


def split(values):
    high = values.astype(jnp.bfloat16)
    return high, (values - high.astype(jnp.float32)).astype(jnp.bfloat16)


def product(a, b):
    return jnp.dot(a, b, preferred_element_type=jnp.float32)


def front_kernel(days, students, perf_hbm, skill_hbm, student_ref, out_ref, perf, skill, proj, sems):
    depth = perf.shape[1] // CHUNKS
    copies = []
    for c in range(CHUNKS):
        part = pl.ds(c * depth, depth)
        one = pltpu.make_async_copy(perf_hbm.at[:, part], perf.at[:, part], sems.at[0, c])
        two = pltpu.make_async_copy(skill_hbm.at[part], skill.at[part], sems.at[1, c])
        one.start()
        two.start()
        copies.append((one, two))
    wide = student_ref[...].astype(jnp.float32)
    total = None
    for c in range(CHUNKS):
        part = pl.ds(c * depth, depth)
        for copy in copies[c]:
            copy.wait()
        term = product(perf[:, part], skill[part])
        total = term if total is None else total + term
    tiles = proj.shape[0]
    for t in range(tiles):
        lanes = pl.ds(t * LANES, LANES)
        proj[t] = total[:, t * LANES : (t + 1) * LANES]
        terms = None
        for s in range(students):
            row = proj[t, pl.ds(s, days, stride=students), :] * wide[s : s + 1, t * LANES : (t + 1) * LANES]
            terms = row if terms is None else terms + row
        out_ref[:days, lanes] = terms
    out_ref[days:, :] = wide


def front(performance, student_factor, skill_factor):
    days, students, skills = performance.shape
    rank = skill_factor.shape[1]
    return pl.pallas_call(
        functools.partial(front_kernel, days, students),
        out_shape=jax.ShapeDtypeStruct((days + students, rank), jnp.float32),
        in_specs=[
            pl.BlockSpec(memory_space=pl.ANY),
            pl.BlockSpec(memory_space=pl.ANY),
            pl.BlockSpec(memory_space=pltpu.VMEM),
        ],
        out_specs=pl.BlockSpec(memory_space=pltpu.VMEM),
        scratch_shapes=[
            pltpu.VMEM((days * students, skills), jnp.bfloat16),
            pltpu.VMEM((skills, rank), jnp.bfloat16),
            pltpu.VMEM((rank // LANES, days * students, LANES), jnp.float32),
            pltpu.SemaphoreType.DMA((2, CHUNKS)),
        ],
        cost_estimate=pl.CostEstimate(
            flops=2 * days * students * skills * rank,
            bytes_accessed=2 * (days * students + rank) * skills,
            transcendentals=0,
        ),
    )(performance.reshape(days * students, skills), skill_factor, student_factor)


def cg_kernel(
    where_ref, coef_ref, mine_ref, other_ref, gram_ref, factor_ref, residual_ref, mttkrp, values, low, high, block
):
    half = mine_ref.shape[0] // 2
    total = 2 * half
    mine = pl.multiple_of(where_ref[0] * half, half)
    other = pl.multiple_of((1 - where_ref[0]) * half, half)
    for place, source in ((mine, mine_ref), (other, other_ref)):
        mttkrp[pl.ds(place, half), :] = source[:half, :]
        values[pl.ds(place, half), :] = source[half:, :]
    gram_high, gram_low = split(gram_ref[...])
    width = gram_ref.shape[1]
    low[:PAD, :] = jnp.zeros((PAD, width), jnp.float32)
    high[pl.ds(total, PAD), :] = jnp.zeros((PAD, width), jnp.float32)
    coef = [coef_ref[l] for l in range(LAGS)]

    def operate(v):
        v_high, v_low = split(v)
        mixed = product(v_high, gram_high) + (product(v_low, gram_high) + product(v_high, gram_low))
        low[pl.ds(PAD, total), :] = v
        ahead = v
        for lag in range(1, LAGS + 1):
            ahead = ahead - coef[lag - 1] * low[pl.ds(PAD - lag, total), :]
        high[:total, :] = ahead
        back = ahead
        for lag in range(1, LAGS + 1):
            back = back - coef[lag - 1] * high[pl.ds(lag, total), :]
        return mixed + smoothing * back

    def inner(a, b):
        return jnp.sum(jnp.sum(a * b, axis=0, keepdims=True), axis=1, keepdims=True)

    factor = values[...]
    residual = mttkrp[...] - operate(factor)
    direction = residual
    now = inner(residual, residual)
    for step in range(ITERS):
        image = operate(direction)
        alpha = now / inner(direction, image)
        factor = factor + alpha * direction
        residual = residual - alpha * image
        if step < ITERS - 1:
            following = inner(residual, residual)
            direction = residual + (following / now) * direction
            now = following
    days, columns = factor_ref.shape
    start = pl.multiple_of(where_ref[1] * days, days)
    for result, target in ((factor, factor_ref), (residual, residual_ref)):
        block[...] = result
        rows = block[pl.ds(start, days), :]
        target[...] = pltpu.roll(rows, where_ref[2], axis=1)[:, :columns]


def conjugate(where, coef, mine, other, gram, days, columns):
    half = mine.shape[0] // 2
    width = gram.shape[1]
    total = 2 * half
    vmem = pl.BlockSpec(memory_space=pltpu.VMEM)
    smem = pl.BlockSpec(memory_space=pltpu.SMEM)
    shape = jax.ShapeDtypeStruct((days, columns), jnp.float32)
    return pl.pallas_call(
        cg_kernel,
        out_shape=(shape, shape),
        in_specs=[smem, smem, vmem, vmem, vmem],
        out_specs=(vmem, vmem),
        scratch_shapes=[
            pltpu.VMEM((total, width), jnp.float32),
            pltpu.VMEM((total, width), jnp.float32),
            pltpu.VMEM((total + PAD, width), jnp.float32),
            pltpu.VMEM((total + PAD, width), jnp.float32),
            pltpu.VMEM((total, width), jnp.float32),
        ],
        cost_estimate=pl.CostEstimate(
            flops=24 * total * width * width, bytes_accessed=4 * width * (width + 2 * total), transcendentals=0
        ),
    )(where, coef, mine, other, gram)


def bits_of(count):
    assert count & (count - 1) == 0 and count > 1
    return [1 << b for b in range(count.bit_length() - 1)]


def local(performance, student_factor, skill_factor, day_prev, ar_coef):
    days, students, _ = performance.shape
    rank = skill_factor.shape[1]
    columns = rank // lax.axis_size("stu")
    payload = front(performance, student_factor, skill_factor)
    skill_gram = lax.dot_general(
        skill_factor, skill_factor, (((0,), (0,)), ((), ())), preferred_element_type=jnp.float32
    )
    for bit in reversed(bits_of(lax.axis_size("stu"))):
        got = exchange(payload, "stu", bit)
        payload = jnp.concatenate([payload[:days] + got[:days], payload[days:], got[days:]], 0)
    student = payload[days:].astype(jnp.bfloat16)
    student_gram = lax.dot_general(
        student, student, (((0,), (0,)), ((), ())), preferred_element_type=jnp.float32
    )
    gram = student_gram * skill_gram
    day = lax.axis_index("day")
    mttkrp, factor = payload[:days], day_prev
    bits = bits_of(lax.axis_size("day"))
    for bit in bits:
        mine = jnp.concatenate([mttkrp, factor], 0)
        other = exchange(mine, "day", bit)
        upper = (day // bit) % 2
        if bit != bits[-1]:
            half = mttkrp.shape[0]
            first = jnp.where(upper == 0, mine, other)
            second = jnp.where(upper == 0, other, mine)
            mttkrp = jnp.concatenate([first[:half], second[:half]], 0)
            factor = jnp.concatenate([first[half:], second[half:]], 0)
    stu = lax.axis_index("stu")
    where = jnp.stack([upper, day, (rank - stu * columns) % rank]).astype(jnp.int32)
    return conjugate(where, ar_coef, mine, other, gram, days, columns)


def solution(mesh):
    return jax.shard_map(
        local,
        mesh=mesh,
        in_specs=(P("day", "stu", None), P("stu", None), P(), P("day", None), P()),
        out_specs=(P("day", "stu"), P("day", "stu")),
        check_vma=False,
    )
```

```python
import functools

import jax
import jax.numpy as jnp
from jax import lax
from jax.experimental import pallas as pl
from jax.experimental.pallas import tpu as pltpu
from jax.sharding import PartitionSpec as P

LAGS = 7
ITERS = 3
PAD = 8
LANES = 128
CHUNKS = 4
VMEM_BYTES = 8 << 20
FRONT_BYTES = 429 << 17


smoothing = 1.0


def exchange(block, mask):
    return lax.ppermute(block, ("day", "stu"), [(i, i ^ mask) for i in range(lax.axis_size(("day", "stu")))])


def split(values):
    high = values.astype(jnp.bfloat16)
    return high, (values - high.astype(jnp.float32)).astype(jnp.bfloat16)


def product(a, b):
    return jnp.dot(a, b, preferred_element_type=jnp.float32)


def front_kernel(days, students, perf_hbm, skill_hbm, student_ref, out_ref, perf, skill, proj, sems):
    depth = perf.shape[1] // CHUNKS
    copies = []
    for c in range(CHUNKS):
        part = pl.ds(c * depth, depth)
        one = pltpu.make_async_copy(perf_hbm.at[:, part], perf.at[:, part], sems.at[0, c])
        two = pltpu.make_async_copy(skill_hbm.at[part], skill.at[part], sems.at[1, c])
        one.start()
        two.start()
        copies.append((one, two))
    wide = student_ref[...].astype(jnp.float32)
    total = None
    for c in range(CHUNKS):
        part = pl.ds(c * depth, depth)
        for copy in copies[c]:
            copy.wait()
        term = product(perf[:, part], skill[part])
        total = term if total is None else total + term
    tiles = proj.shape[0]
    for t in range(tiles):
        lanes = pl.ds(t * LANES, LANES)
        proj[t] = total[:, t * LANES : (t + 1) * LANES]
        terms = None
        for s in range(students):
            row = proj[t, pl.ds(s, days, stride=students), :] * wide[s : s + 1, t * LANES : (t + 1) * LANES]
            terms = row if terms is None else terms + row
        out_ref[:days, lanes] = terms
    out_ref[days:, :] = wide


def front(performance, student_factor, skill_factor):
    days, students, skills = performance.shape
    rank = skill_factor.shape[1]
    return pl.pallas_call(
        functools.partial(front_kernel, days, students),
        compiler_params=pltpu.CompilerParams(vmem_limit_bytes=FRONT_BYTES),
        out_shape=jax.ShapeDtypeStruct((days + students, rank), jnp.float32),
        in_specs=[
            pl.BlockSpec(memory_space=pltpu.HBM),
            pl.BlockSpec(memory_space=pltpu.HBM),
            pl.BlockSpec(memory_space=pltpu.VMEM),
        ],
        out_specs=pl.BlockSpec(memory_space=pltpu.VMEM),
        scratch_shapes=[
            pltpu.VMEM((days * students, skills), jnp.bfloat16),
            pltpu.VMEM((skills, rank), jnp.bfloat16),
            pltpu.VMEM((rank // LANES, days * students, LANES), jnp.float32),
            pltpu.SemaphoreType.DMA((2, CHUNKS)),
        ],
        cost_estimate=pl.CostEstimate(
            flops=2 * days * students * skills * rank,
            bytes_accessed=2 * (days * students + rank) * skills,
            transcendentals=0,
        ),
    )(performance.reshape(days * students, skills), skill_factor, student_factor)


def cg_kernel(
    where_ref, coef_ref, mine_ref, other_ref, gram_ref, factor_ref, residual_ref, mttkrp, values, low, high, block
):
    half = mine_ref.shape[0] // 2
    total = 2 * half
    mine = pl.multiple_of(where_ref[0] * half, half)
    other = pl.multiple_of((1 - where_ref[0]) * half, half)
    for place, source in ((mine, mine_ref), (other, other_ref)):
        mttkrp[pl.ds(place, half), :] = source[:half, :]
        values[pl.ds(place, half), :] = source[half:, :]
    gram_high, gram_low = split(gram_ref[...])
    width = gram_ref.shape[1]
    low[:PAD, :] = jnp.zeros((PAD, width), jnp.float32)
    high[pl.ds(total, PAD), :] = jnp.zeros((PAD, width), jnp.float32)
    coef = [coef_ref[l] for l in range(LAGS)]

    def operate(v):
        v_high, v_low = split(v)
        mixed = product(v_high, gram_high) + (product(v_low, gram_high) + product(v_high, gram_low))
        low[pl.ds(PAD, total), :] = v
        ahead = v
        for lag in range(1, LAGS + 1):
            ahead = ahead - coef[lag - 1] * low[pl.ds(PAD - lag, total), :]
        high[:total, :] = ahead
        back = ahead
        for lag in range(1, LAGS + 1):
            back = back - coef[lag - 1] * high[pl.ds(lag, total), :]
        return mixed + smoothing * back

    def inner(a, b):
        return jnp.sum(jnp.sum(a * b, axis=0, keepdims=True), axis=1, keepdims=True)

    factor = values[...]
    residual = mttkrp[...] - operate(factor)
    direction = residual
    now = inner(residual, residual)
    for step in range(ITERS):
        image = operate(direction)
        alpha = now / inner(direction, image)
        factor = factor + alpha * direction
        residual = residual - alpha * image
        if step < ITERS - 1:
            following = inner(residual, residual)
            direction = residual + (following / now) * direction
            now = following
    columns, days = factor_ref.shape
    start = pl.multiple_of(where_ref[1] * days, days)
    for result, target in ((factor, factor_ref), (residual, residual_ref)):
        block[...] = result
        rows = block[pl.ds(start, days), :]
        target[...] = pltpu.roll(rows, where_ref[2], axis=1)[:, :columns].T


def conjugate(where, coef, mine, other, gram, days, columns):
    half = mine.shape[0] // 2
    width = gram.shape[1]
    total = 2 * half
    vmem = pl.BlockSpec(memory_space=pltpu.VMEM)
    smem = pl.BlockSpec(memory_space=pltpu.SMEM)
    shape = jax.ShapeDtypeStruct((columns, days), jnp.float32)
    return pl.pallas_call(
        cg_kernel,
        compiler_params=pltpu.CompilerParams(vmem_limit_bytes=VMEM_BYTES),
        out_shape=(shape, shape),
        in_specs=[smem, smem, vmem, vmem, vmem],
        out_specs=(vmem, vmem),
        scratch_shapes=[
            pltpu.VMEM((total, width), jnp.float32),
            pltpu.VMEM((total, width), jnp.float32),
            pltpu.VMEM((total + PAD, width), jnp.float32),
            pltpu.VMEM((total + PAD, width), jnp.float32),
            pltpu.VMEM((total, width), jnp.float32),
        ],
        cost_estimate=pl.CostEstimate(
            flops=24 * total * width * width, bytes_accessed=4 * width * (width + 2 * total), transcendentals=0
        ),
    )(where, coef, mine, other, gram)


def bits_of(count):
    assert count & (count - 1) == 0 and count > 1
    return [1 << b for b in range(count.bit_length() - 1)]


def local(performance, student_factor, skill_factor, day_prev, ar_coef):
    days, students, _ = performance.shape
    rank = skill_factor.shape[1]
    columns = rank // lax.axis_size("stu")
    payload = front(performance, student_factor, skill_factor)
    skill_gram = lax.dot_general(
        skill_factor, skill_factor, (((0,), (0,)), ((), ())), preferred_element_type=jnp.float32
    )
    stu_size, day_size = lax.axis_size("stu"), lax.axis_size("day")
    for bit in reversed(bits_of(stu_size)):
        got = exchange(payload, bit | 1)
        payload = jnp.concatenate([payload[:days] + got[:days], payload[days:], got[days:]], 0)
    student = payload[days:].astype(jnp.bfloat16)
    student_gram = lax.dot_general(
        student, student, (((0,), (0,)), ((), ())), preferred_element_type=jnp.float32
    )
    gram = student_gram * skill_gram
    day = lax.axis_index("day")
    mttkrp, factor = payload[:days], day_prev
    bits = bits_of(day_size)
    for bit in bits:
        mine = jnp.concatenate([mttkrp, factor], 0)
        other = exchange(mine, bit * stu_size + 1)
        upper = (day // bit) % 2
        if bit != bits[-1]:
            half = mttkrp.shape[0]
            first = jnp.where(upper == 0, mine, other)
            second = jnp.where(upper == 0, other, mine)
            mttkrp = jnp.concatenate([first[:half], second[:half]], 0)
            factor = jnp.concatenate([first[half:], second[half:]], 0)
    stu = lax.axis_index("stu")
    where = jnp.stack([upper, day, (rank - stu * columns) % rank]).astype(jnp.int32)
    factor, residual = conjugate(where, ar_coef, mine, other, gram, days, columns)
    return factor.T, residual.T


def solution(mesh):
    return jax.shard_map(
        local,
        mesh=mesh,
        in_specs=(P("day", "stu", None), P("stu", None), P(), P("day", None), P()),
        out_specs=(P("day", "stu"), P("day", "stu")),
        check_vma=False,
    )
```

```python
import functools

import jax
import jax.numpy as jnp
from jax import lax
from jax.experimental import pallas as pl
from jax.experimental.pallas import tpu as pltpu
from jax.sharding import PartitionSpec as P

LAGS = 7
ITERS = 3
PAD = 8
LANES = 128
VMEM_BYTES = 8 << 20


smoothing = 1.0

VMEM = pl.BlockSpec(memory_space=pltpu.VMEM)
HBM = pl.BlockSpec(memory_space=pltpu.HBM)


def exchange(block, mask):
    return lax.ppermute(block, ("day", "stu"), [(i, i ^ mask) for i in range(lax.axis_size(("day", "stu")))])


def own_part():
    place = lax.axis_index("day") ^ lax.axis_index("stu")
    for shift in (8, 4, 2, 1):
        place = place ^ (place >> shift)
    return place & 1


def split(values):
    high = values.astype(jnp.bfloat16)
    return high, (values - high.astype(jnp.float32)).astype(jnp.bfloat16)


def product(a, b):
    return jnp.dot(a, b, preferred_element_type=jnp.float32)


def student_sums(perf, skill, wide, proj, out_ref):
    students = wide.shape[0]
    total = product(perf[...], skill[...])
    days = total.shape[0] // students
    for t in range(proj.shape[0]):
        lanes = slice(t * LANES, (t + 1) * LANES)
        proj[t] = total[:, lanes]
        terms = None
        for s in range(students):
            row = proj[t, pl.ds(s, days, stride=students), :] * wide[s : s + 1, lanes]
            terms = row if terms is None else terms + row
        out_ref[:days, lanes] = terms


def send_kernel(perf_hbm, skill_hbm, student_hbm, send_ref, skill, keep, student, perf, proj, sems):
    rows = perf.shape[0]
    part = own_part()
    away = perf_hbm.at[pl.ds(pl.multiple_of((1 - part) * rows, rows), rows)]
    home = perf_hbm.at[pl.ds(pl.multiple_of(part * rows, rows), rows)]
    copies = []
    for i, (source, target) in enumerate(
        ((student_hbm, student), (skill_hbm, skill), (away, perf), (home, keep))
    ):
        copies.append(pltpu.make_async_copy(source, target, sems.at[i]))
        copies[i].start()
    for copy in copies[:3]:
        copy.wait()
    student_sums(perf, skill, student[...].astype(jnp.float32), proj, send_ref)
    copies[3].wait()


def send_part(performance, student_factor, skill_factor):
    days, students, skills = performance.shape
    rank = skill_factor.shape[1]
    rows = days * students // 2
    operands = performance.reshape(2 * rows, skills), skill_factor, student_factor
    return pl.pallas_call(
        send_kernel,
        compiler_params=pltpu.CompilerParams(vmem_limit_bytes=VMEM_BYTES),
        out_shape=(
            jax.ShapeDtypeStruct((days // 2, rank), jnp.float32),
            jax.ShapeDtypeStruct((skills, rank), jnp.bfloat16),
            jax.ShapeDtypeStruct((rows, skills), jnp.bfloat16),
            jax.ShapeDtypeStruct((students, rank), jnp.bfloat16),
        ),
        in_specs=[HBM] * 3,
        out_specs=(VMEM,) * 4,
        scratch_shapes=[
            pltpu.VMEM((rows, skills), jnp.bfloat16),
            pltpu.VMEM((rank // LANES, rows, LANES), jnp.float32),
            pltpu.SemaphoreType.DMA((4,)),
        ],
        cost_estimate=pl.CostEstimate(
            flops=2 * rows * skills * rank, bytes_accessed=2 * (2 * rows + rank) * skills, transcendentals=0
        ),
    )(*(pltpu.with_memory_space_constraint(x, pltpu.HBM) for x in operands))


def keep_kernel(perf, skill, student, keep_ref, proj):
    wide = student[...].astype(jnp.float32)
    student_sums(perf, skill, wide, proj, keep_ref)
    keep_ref[-wide.shape[0] :, :] = wide


def keep_part(perf, skill, student):
    rows, skills = perf.shape
    students, rank = student.shape
    return pl.pallas_call(
        keep_kernel,
        compiler_params=pltpu.CompilerParams(vmem_limit_bytes=VMEM_BYTES),
        out_shape=jax.ShapeDtypeStruct((rows // students + students, rank), jnp.float32),
        in_specs=[VMEM] * 3,
        out_specs=VMEM,
        scratch_shapes=[pltpu.VMEM((rank // LANES, rows, LANES), jnp.float32)],
        cost_estimate=pl.CostEstimate(
            flops=2 * rows * skills * rank, bytes_accessed=2 * (rows + rank) * skills, transcendentals=0
        ),
    )(perf, skill, student)


def cg_kernel(
    columns, coef_ref, prev_ref, mine_ref, other_ref, skill_gram_ref, factor_hbm, residual_hbm,
    mttkrp, values, low, high, block, results, sems,
):
    days, width = prev_ref.shape
    total = mttkrp.shape[0]
    blocks, half = total // days, days // 2
    day, stu, part = lax.axis_index("day"), lax.axis_index("stu"), own_part()
    values[pl.ds(pl.multiple_of(day * days, days), days), :] = prev_ref[...]
    for source, at in ((mine_ref, part), (other_ref, 1 - part)):
        for b in range(blocks):
            place = pl.ds(pl.multiple_of((day ^ b) * days + at * half, half), half)
            mttkrp[place, :] = source[b * half : (b + 1) * half, :]
            if b > 0:
                row = (blocks + b - 1) * half
                values[place, :] = source[row : row + half, :]
    start = (2 * blocks - 1) * half
    students = jnp.concatenate([mine_ref[start:, :], other_ref[start:, :]], 0).astype(jnp.bfloat16)
    student_gram = lax.dot_general(
        students, students, (((0,), (0,)), ((), ())), preferred_element_type=jnp.float32
    )
    gram_high, gram_low = split(student_gram * skill_gram_ref[...])
    gram = jnp.concatenate([gram_high, gram_high, gram_low], 0)
    low[:PAD, :] = jnp.zeros((PAD, width), jnp.float32)
    high[pl.ds(total, PAD), :] = jnp.zeros((PAD, width), jnp.float32)
    coef = [coef_ref[:, l : l + 1] for l in range(LAGS)]

    def operate(v):
        v_high, v_low = split(v)
        mixed = product(jnp.concatenate([v_high, v_low, v_high], 1), gram)
        low[pl.ds(PAD, total), :] = v
        ahead = v
        for lag in range(1, LAGS + 1):
            ahead = ahead - coef[lag - 1] * low[pl.ds(PAD - lag, total), :]
        high[:total, :] = ahead
        back = ahead
        for lag in range(1, LAGS + 1):
            back = back - coef[lag - 1] * high[pl.ds(lag, total), :]
        return mixed + smoothing * back

    def inner(a, b):
        return jnp.sum(jnp.sum(a * b, axis=0, keepdims=True), axis=1, keepdims=True)

    factor = values[...]
    residual = mttkrp[...] - operate(factor)
    direction = residual
    now = inner(residual, residual)
    for step in range(ITERS):
        image = operate(direction)
        alpha = now / inner(direction, image)
        factor = factor + alpha * direction
        residual = residual - alpha * image
        if step < ITERS - 1:
            following = inner(residual, residual)
            direction = residual + (following / now) * direction
            now = following
    start = pl.multiple_of(day * days, days)
    turn = jnp.where(stu == 0, 0, width - stu * columns)
    copies = []
    for i, (result, target) in enumerate(((factor, factor_hbm), (residual, residual_hbm))):
        block[i] = result
        rows = block[i, pl.ds(start, days), :]
        results[i] = pltpu.roll(rows, turn, axis=1)[:, :columns].T
        copies.append(pltpu.make_async_copy(results.at[i], target, sems.at[i]))
        copies[i].start()
    for copy in copies:
        copy.wait()


def conjugate(coef, prev, mine, other, skill_gram, blocks, columns):
    days, width = prev.shape
    total = days * blocks
    shape = jax.ShapeDtypeStruct((columns, days), jnp.float32)
    return pl.pallas_call(
        functools.partial(cg_kernel, columns),
        compiler_params=pltpu.CompilerParams(vmem_limit_bytes=VMEM_BYTES),
        out_shape=(shape, shape),
        in_specs=[VMEM] * 5,
        out_specs=(HBM, HBM),
        scratch_shapes=[
            pltpu.VMEM((total, width), jnp.float32),
            pltpu.VMEM((total, width), jnp.float32),
            pltpu.VMEM((total + PAD, width), jnp.float32),
            pltpu.VMEM((total + PAD, width), jnp.float32),
            pltpu.VMEM((2, total, width), jnp.float32),
            pltpu.VMEM((2, columns, days), jnp.float32),
            pltpu.SemaphoreType.DMA((2,)),
        ],
        cost_estimate=pl.CostEstimate(
            flops=24 * total * width * width, bytes_accessed=4 * width * (width + 2 * total), transcendentals=0
        ),
    )(coef.reshape(1, LAGS), prev, mine, other, skill_gram)


def bits_of(count):
    assert count & (count - 1) == 0 and count > 1
    return [1 << b for b in range(count.bit_length() - 1)]


def local(performance, student_factor, skill_factor, day_prev, ar_coef):
    days = performance.shape[0]
    half = days // 2
    rank = skill_factor.shape[1]
    stu_size, day_size = lax.axis_size("stu"), lax.axis_size("day")
    send, skill, perf, student = send_part(performance, student_factor, skill_factor)
    got = exchange(send, 1)
    keep = keep_part(perf, skill, student)
    skill_gram = lax.dot_general(skill, skill, (((0,), (0,)), ((), ())), preferred_element_type=jnp.float32)
    payload = jnp.concatenate([keep[:half] + got, keep[half:]], 0)
    for bit in bits_of(stu_size)[:0:-1]:
        got = exchange(payload, bit | 1)
        payload = jnp.concatenate([payload[:half] + got[:half], payload[half:], got[half:]], 0)
    mttkrp, students = payload[:half], payload[half:]
    factor = lax.dynamic_slice_in_dim(day_prev, own_part() * half, half, 0)
    for bit in bits_of(day_size):
        got = exchange(jnp.concatenate([mttkrp, factor], 0), bit * stu_size + 1)
        rows = bit * half
        mttkrp = jnp.concatenate([mttkrp, got[:rows]], 0)
        factor = jnp.concatenate([factor, got[rows:]], 0)
    mine = jnp.concatenate([mttkrp, factor[half:], students], 0)
    other = exchange(mine, 1)
    factor, residual = conjugate(ar_coef, day_prev, mine, other, skill_gram, day_size, rank // stu_size)
    return factor.T, residual.T


def solution(mesh):
    return jax.shard_map(
        local,
        mesh=mesh,
        in_specs=(P("day", "stu", None), P("stu", None), P(), P("day", None), P()),
        out_specs=(P("day", "stu"), P("day", "stu")),
        check_vma=False,
    )
```

```python
import functools

import jax
import jax.numpy as jnp
from jax import lax
from jax.experimental import pallas as pl
from jax.experimental.pallas import tpu as pltpu
from jax.sharding import PartitionSpec as P

LAGS = 7
ITERS = 3
PAD = 8
LANES = 128
VMEM_BYTES = 8 << 20


smoothing = 1.0

VMEM = pl.BlockSpec(memory_space=pltpu.VMEM)
HBM = pl.BlockSpec(memory_space=pltpu.HBM)


def exchange(block, mask, other=None):
    both = mask, mask if other is None else other
    union = both[0] | both[1]
    route = [(i, i ^ both[(i & union).bit_count() % 2]) for i in range(lax.axis_size(("day", "stu")))]
    return lax.ppermute(block, ("day", "stu"), route)


def own_part():
    place = lax.axis_index("day") ^ lax.axis_index("stu")
    for shift in (8, 4, 2, 1):
        place = place ^ (place >> shift)
    return place & 1


def split(values):
    high = values.astype(jnp.bfloat16)
    return high, (values - high.astype(jnp.float32)).astype(jnp.bfloat16)


def product(a, b):
    return jnp.dot(a, b, preferred_element_type=jnp.float32)


def student_sums(perf, skill, wide, proj, out_ref):
    students = wide.shape[0]
    total = product(perf[...], skill[...])
    days = total.shape[0] // students
    for t in range(proj.shape[0]):
        lanes = slice(t * LANES, (t + 1) * LANES)
        proj[t] = total[:, lanes]
        terms = None
        for s in range(students):
            row = proj[t, pl.ds(s, days, stride=students), :] * wide[s : s + 1, lanes]
            terms = row if terms is None else terms + row
        out_ref[:days, lanes] = terms


def send_kernel(perf_hbm, skill_hbm, student_hbm, send_ref, skill, keep, student, perf, proj, sems):
    rows = perf.shape[0]
    part = own_part()
    away = perf_hbm.at[pl.ds(pl.multiple_of((1 - part) * rows, rows), rows)]
    home = perf_hbm.at[pl.ds(pl.multiple_of(part * rows, rows), rows)]
    copies = []
    for i, (source, target) in enumerate(
        ((student_hbm, student), (skill_hbm, skill), (away, perf), (home, keep))
    ):
        copies.append(pltpu.make_async_copy(source, target, sems.at[i]))
        copies[i].start()
    for copy in copies[:3]:
        copy.wait()
    student_sums(perf, skill, student[...].astype(jnp.float32), proj, send_ref)
    copies[3].wait()


def send_part(performance, student_factor, skill_factor):
    days, students, skills = performance.shape
    rank = skill_factor.shape[1]
    rows = days * students // 2
    operands = performance.reshape(2 * rows, skills), skill_factor, student_factor
    return pl.pallas_call(
        send_kernel,
        compiler_params=pltpu.CompilerParams(vmem_limit_bytes=VMEM_BYTES),
        out_shape=(
            jax.ShapeDtypeStruct((days // 2, rank), jnp.float32),
            jax.ShapeDtypeStruct((skills, rank), jnp.bfloat16),
            jax.ShapeDtypeStruct((rows, skills), jnp.bfloat16),
            jax.ShapeDtypeStruct((students, rank), jnp.bfloat16),
        ),
        in_specs=[HBM] * 3,
        out_specs=(VMEM,) * 4,
        scratch_shapes=[
            pltpu.VMEM((rows, skills), jnp.bfloat16),
            pltpu.VMEM((rank // LANES, rows, LANES), jnp.float32),
            pltpu.SemaphoreType.DMA((4,)),
        ],
        cost_estimate=pl.CostEstimate(
            flops=2 * rows * skills * rank, bytes_accessed=2 * (2 * rows + rank) * skills, transcendentals=0
        ),
    )(*(pltpu.with_memory_space_constraint(x, pltpu.HBM) for x in operands))


def keep_kernel(perf, skill, student, keep_ref, proj):
    wide = student[...].astype(jnp.float32)
    student_sums(perf, skill, wide, proj, keep_ref)
    keep_ref[-wide.shape[0] :, :] = wide


def keep_part(perf, skill, student):
    rows, skills = perf.shape
    students, rank = student.shape
    return pl.pallas_call(
        keep_kernel,
        compiler_params=pltpu.CompilerParams(vmem_limit_bytes=VMEM_BYTES),
        out_shape=jax.ShapeDtypeStruct((rows // students + students, rank), jnp.float32),
        in_specs=[VMEM] * 3,
        out_specs=VMEM,
        scratch_shapes=[pltpu.VMEM((rank // LANES, rows, LANES), jnp.float32)],
        cost_estimate=pl.CostEstimate(
            flops=2 * rows * skills * rank, bytes_accessed=2 * (rows + rank) * skills, transcendentals=0
        ),
    )(perf, skill, student)


def cg_kernel(
    columns, coef_ref, prev_ref, mine_ref, other_ref, skill_gram_ref, factor_hbm, residual_hbm,
    mttkrp, values, low, high, block, results, sems,
):
    days, width = prev_ref.shape
    total = mttkrp.shape[0]
    blocks, half = total // days, days // 2
    day, stu, part = lax.axis_index("day"), lax.axis_index("stu"), own_part()
    values[pl.ds(pl.multiple_of(day * days, days), days), :] = prev_ref[...]
    for source, at in ((mine_ref, part), (other_ref, 1 - part)):
        for b in range(blocks):
            place = pl.ds(pl.multiple_of((day ^ b) * days + at * half, half), half)
            mttkrp[place, :] = source[b * half : (b + 1) * half, :]
            if b > 0:
                row = (blocks + b - 1) * half
                values[place, :] = source[row : row + half, :]
    start = (2 * blocks - 1) * half
    students = jnp.concatenate([mine_ref[start:, :], other_ref[start:, :]], 0).astype(jnp.bfloat16)
    student_gram = lax.dot_general(
        students, students, (((0,), (0,)), ((), ())), preferred_element_type=jnp.float32
    )
    gram_high, gram_low = split(student_gram * skill_gram_ref[...])
    gram = jnp.concatenate([gram_high, gram_high, gram_low], 0)
    low[:PAD, :] = jnp.zeros((PAD, width), jnp.float32)
    high[pl.ds(total, PAD), :] = jnp.zeros((PAD, width), jnp.float32)
    coef = [coef_ref[:, l : l + 1] for l in range(LAGS)]

    def operate(v):
        v_high, v_low = split(v)
        mixed = product(jnp.concatenate([v_high, v_low, v_high], 1), gram)
        low[pl.ds(PAD, total), :] = v
        ahead = v
        for lag in range(1, LAGS + 1):
            ahead = ahead - coef[lag - 1] * low[pl.ds(PAD - lag, total), :]
        high[:total, :] = ahead
        back = ahead
        for lag in range(1, LAGS + 1):
            back = back - coef[lag - 1] * high[pl.ds(lag, total), :]
        return mixed + smoothing * back

    def inner(a, b):
        terms = a * b
        tiles = [
            terms[i : i + PAD, j : j + LANES] for i in range(0, total, PAD) for j in range(0, width, LANES)
        ]
        while len(tiles) > 1:
            tiles = [x + y for x, y in zip(tiles[::2], tiles[1::2], strict=True)]
        return jnp.sum(jnp.sum(tiles[0], axis=1, keepdims=True), axis=0, keepdims=True)

    factor = values[...]
    residual = mttkrp[...] - operate(factor)
    direction, image = residual, operate(residual)
    now = inner(residual, residual)
    for step in range(ITERS):
        alpha = now / inner(direction, image)
        factor = factor + alpha * direction
        residual = residual - alpha * image
        if step < ITERS - 1:
            ahead, following = operate(residual), inner(residual, residual)
            beta = following / now
            direction = residual + beta * direction
            image = ahead + beta * image
            now = following
    start = pl.multiple_of(day * days, days)
    turn = jnp.where(stu == 0, 0, width - stu * columns)
    copies = []
    for i, (result, target) in enumerate(((factor, factor_hbm), (residual, residual_hbm))):
        block[i] = result
        rows = block[i, pl.ds(start, days), :]
        results[i] = pltpu.roll(rows, turn, axis=1)[:, :columns].T
        copies.append(pltpu.make_async_copy(results.at[i], target, sems.at[i]))
        copies[i].start()
    for copy in copies:
        copy.wait()


def conjugate(coef, prev, mine, other, skill_gram, blocks, columns):
    days, width = prev.shape
    total = days * blocks
    shape = jax.ShapeDtypeStruct((columns, days), jnp.float32)
    return pl.pallas_call(
        functools.partial(cg_kernel, columns),
        compiler_params=pltpu.CompilerParams(vmem_limit_bytes=VMEM_BYTES),
        out_shape=(shape, shape),
        in_specs=[VMEM] * 5,
        out_specs=(HBM, HBM),
        scratch_shapes=[
            pltpu.VMEM((total, width), jnp.float32),
            pltpu.VMEM((total, width), jnp.float32),
            pltpu.VMEM((total + PAD, width), jnp.float32),
            pltpu.VMEM((total + PAD, width), jnp.float32),
            pltpu.VMEM((2, total, width), jnp.float32),
            pltpu.VMEM((2, columns, days), jnp.float32),
            pltpu.SemaphoreType.DMA((2,)),
        ],
        cost_estimate=pl.CostEstimate(
            flops=24 * total * width * width, bytes_accessed=4 * width * (width + 2 * total), transcendentals=0
        ),
    )(coef.reshape(1, LAGS), prev, mine, other, skill_gram)


def bits_of(count):
    assert count & (count - 1) == 0 and count > 1
    return [1 << b for b in range(count.bit_length() - 1)]


def local(performance, student_factor, skill_factor, day_prev, ar_coef):
    days = performance.shape[0]
    half = days // 2
    rank = skill_factor.shape[1]
    stu_size, day_size = lax.axis_size("stu"), lax.axis_size("day")
    send, skill, perf, student = send_part(performance, student_factor, skill_factor)
    got = exchange(send, 1)
    keep = keep_part(perf, skill, student)
    skill_gram = lax.dot_general(skill, skill, (((0,), (0,)), ((), ())), preferred_element_type=jnp.float32)
    payload = jnp.concatenate([keep[:half] + got, keep[half:]], 0)
    masks = [bit | 1 for bit in bits_of(stu_size)[:0:-1]]
    for mask, other in zip(masks, masks[:-2] + masks[:-3:-1], strict=True):
        got = exchange(payload, mask, other)
        payload = jnp.concatenate([payload[:half] + got[:half], payload[half:], got[half:]], 0)
    mttkrp, students = payload[:half], payload[half:]
    factor = lax.dynamic_slice_in_dim(day_prev, own_part() * half, half, 0)
    for bit in bits_of(day_size):
        got = exchange(jnp.concatenate([mttkrp, factor], 0), bit * stu_size + 1)
        rows = bit * half
        mttkrp = jnp.concatenate([mttkrp, got[:rows]], 0)
        factor = jnp.concatenate([factor, got[rows:]], 0)
    mine = jnp.concatenate([mttkrp, factor[half:], students], 0)
    other = exchange(mine, 1)
    factor, residual = conjugate(ar_coef, day_prev, mine, other, skill_gram, day_size, rank // stu_size)
    return factor.T, residual.T


def solution(mesh):
    return jax.shard_map(
        local,
        mesh=mesh,
        in_specs=(P("day", "stu", None), P("stu", None), P(), P("day", None), P()),
        out_specs=(P("day", "stu"), P("day", "stu")),
        check_vma=False,
    )
```

```python
import functools

import jax
import jax.numpy as jnp
from jax import lax
from jax.experimental import pallas as pl
from jax.experimental.pallas import tpu as pltpu
from jax.sharding import PartitionSpec as P

LAGS = 7
ITERS = 3
PAD = 8
LANES = 128
VMEM_BYTES = 8 << 20


smoothing = 1.0

VMEM = pl.BlockSpec(memory_space=pltpu.VMEM)
HBM = pl.BlockSpec(memory_space=pltpu.HBM)


def exchange(block, mask, other=None):
    both = mask, mask if other is None else other
    union = both[0] | both[1]
    route = [(i, i ^ both[(i & union).bit_count() % 2]) for i in range(lax.axis_size(("day", "stu")))]
    return lax.ppermute(block, ("day", "stu"), route)


def own_part():
    place = lax.axis_index("day") ^ lax.axis_index("stu")
    for shift in (8, 4, 2, 1):
        place = place ^ (place >> shift)
    return place & 1


def split(values):
    high = values.astype(jnp.bfloat16)
    return high, (values - high.astype(jnp.float32)).astype(jnp.bfloat16)


def product(a, b):
    return jnp.dot(a, b, preferred_element_type=jnp.float32)


def student_sums(perf, skill, wide, proj, out_ref):
    students = wide.shape[0]
    total = product(perf[...], skill[...])
    days = total.shape[0] // students
    for t in range(proj.shape[0]):
        lanes = slice(t * LANES, (t + 1) * LANES)
        proj[t] = total[:, lanes]
        terms = None
        for s in range(students):
            row = proj[t, pl.ds(s, days, stride=students), :] * wide[s : s + 1, lanes]
            terms = row if terms is None else terms + row
        out_ref[:days, lanes] = terms


def send_kernel(perf_hbm, skill_hbm, student_hbm, send_ref, skill, keep, student, perf, proj, sems):
    rows = perf.shape[0]
    part = own_part()
    away = perf_hbm.at[pl.ds(pl.multiple_of((1 - part) * rows, rows), rows)]
    home = perf_hbm.at[pl.ds(pl.multiple_of(part * rows, rows), rows)]
    copies = []
    for i, (source, target) in enumerate(
        ((student_hbm, student), (skill_hbm, skill), (away, perf), (home, keep))
    ):
        copies.append(pltpu.make_async_copy(source, target, sems.at[i]))
        copies[i].start()
    for copy in copies[:3]:
        copy.wait()
    student_sums(perf, skill, student[...].astype(jnp.float32), proj, send_ref)
    copies[3].wait()


def send_part(performance, student_factor, skill_factor):
    days, students, skills = performance.shape
    rank = skill_factor.shape[1]
    rows = days * students // 2
    operands = performance.reshape(2 * rows, skills), skill_factor, student_factor
    return pl.pallas_call(
        send_kernel,
        compiler_params=pltpu.CompilerParams(vmem_limit_bytes=VMEM_BYTES),
        out_shape=(
            jax.ShapeDtypeStruct((days // 2, rank), jnp.float32),
            jax.ShapeDtypeStruct((skills, rank), jnp.bfloat16),
            jax.ShapeDtypeStruct((rows, skills), jnp.bfloat16),
            jax.ShapeDtypeStruct((students, rank), jnp.bfloat16),
        ),
        in_specs=[HBM] * 3,
        out_specs=(VMEM,) * 4,
        scratch_shapes=[
            pltpu.VMEM((rows, skills), jnp.bfloat16),
            pltpu.VMEM((rank // LANES, rows, LANES), jnp.float32),
            pltpu.SemaphoreType.DMA((4,)),
        ],
        cost_estimate=pl.CostEstimate(
            flops=2 * rows * skills * rank, bytes_accessed=2 * (2 * rows + rank) * skills, transcendentals=0
        ),
    )(*(pltpu.with_memory_space_constraint(x, pltpu.HBM) for x in operands))


def keep_kernel(perf, skill, student, prev_hbm, coef_hbm, keep_ref, prev, coef, proj, sems):
    copies = [
        pltpu.make_async_copy(prev_hbm, prev, sems.at[0]),
        pltpu.make_async_copy(coef_hbm, coef, sems.at[1]),
    ]
    for copy in copies:
        copy.start()
    wide = student[...].astype(jnp.float32)
    student_sums(perf, skill, wide, proj, keep_ref)
    keep_ref[-wide.shape[0] :, :] = wide
    for copy in copies:
        copy.wait()


def keep_part(perf, skill, student, prev, coef):
    rows, skills = perf.shape
    students, rank = student.shape
    small = prev, coef.reshape(1, LAGS)
    return pl.pallas_call(
        keep_kernel,
        compiler_params=pltpu.CompilerParams(vmem_limit_bytes=VMEM_BYTES),
        out_shape=(
            jax.ShapeDtypeStruct((rows // students + students, rank), jnp.float32),
            *(jax.ShapeDtypeStruct(x.shape, x.dtype) for x in small),
        ),
        in_specs=[VMEM] * 3 + [HBM] * 2,
        out_specs=(VMEM,) * 3,
        scratch_shapes=[
            pltpu.VMEM((rank // LANES, rows, LANES), jnp.float32),
            pltpu.SemaphoreType.DMA((2,)),
        ],
        cost_estimate=pl.CostEstimate(
            flops=2 * rows * skills * rank, bytes_accessed=2 * (rows + rank) * skills, transcendentals=0
        ),
    )(perf, skill, student, *(pltpu.with_memory_space_constraint(x, pltpu.HBM) for x in small))


def gram_kernel(mine_ref, other_ref, skill_gram_ref, out_ref):
    students = jnp.concatenate([mine_ref[...], other_ref[...]], 0).astype(jnp.bfloat16)
    student_gram = lax.dot_general(
        students, students, (((0,), (0,)), ((), ())), preferred_element_type=jnp.float32
    )
    rank = out_ref.shape[0]
    high, low = split(student_gram * skill_gram_ref[...])
    out_ref[:, :rank] = high
    out_ref[:, rank:] = low


def gram_stack(mine, other, skill_gram):
    count, rank = mine.shape
    return pl.pallas_call(
        gram_kernel,
        compiler_params=pltpu.CompilerParams(vmem_limit_bytes=VMEM_BYTES),
        out_shape=jax.ShapeDtypeStruct((rank, 2 * rank), jnp.bfloat16),
        in_specs=[VMEM] * 3,
        out_specs=VMEM,
        cost_estimate=pl.CostEstimate(
            flops=4 * count * rank * rank, bytes_accessed=8 * rank * rank, transcendentals=0
        ),
    )(mine, other, skill_gram)


def cg_kernel(
    columns, coef_ref, prev_ref, mine_ref, other_ref, gram_ref, factor_hbm, residual_hbm,
    mttkrp, values, low, high, block, results, sems,
):
    days, width = prev_ref.shape
    total = mttkrp.shape[0]
    blocks, half = total // days, days // 2
    day, stu, part = lax.axis_index("day"), lax.axis_index("stu"), own_part()
    values[pl.ds(pl.multiple_of(day * days, days), days), :] = prev_ref[...]
    for source, at in ((mine_ref, part), (other_ref, 1 - part)):
        for b in range(blocks):
            place = pl.ds(pl.multiple_of((day ^ b) * days + at * half, half), half)
            mttkrp[place, :] = source[b * half : (b + 1) * half, :]
            if b > 0:
                row = (blocks + b - 1) * half
                values[place, :] = source[row : row + half, :]
    gram_high, gram_wide = gram_ref[:, :width], gram_ref[...]
    low[:PAD, :] = jnp.zeros((PAD, width), jnp.float32)
    high[pl.ds(total, PAD), :] = jnp.zeros((PAD, width), jnp.float32)
    coef = [coef_ref[:, l : l + 1] for l in range(LAGS)]

    def operate(v):
        v_high, v_low = split(v)
        both = product(jnp.concatenate([v_high, v_low], 0), gram_wide)
        mixed = both[:total, :width] + (both[total:, :width] + both[:total, width:])
        low[pl.ds(PAD, total), :] = v
        ahead = v
        for lag in range(1, LAGS + 1):
            ahead = ahead - coef[lag - 1] * low[pl.ds(PAD - lag, total), :]
        high[:total, :] = ahead
        back = ahead
        for lag in range(1, LAGS + 1):
            back = back - coef[lag - 1] * high[pl.ds(lag, total), :]
        return mixed + smoothing * back

    def inner(a, b):
        terms = a * b
        tiles = [
            terms[i : i + PAD, j : j + LANES] for i in range(0, total, PAD) for j in range(0, width, LANES)
        ]
        while len(tiles) > 1:
            tiles = [x + y for x, y in zip(tiles[::2], tiles[1::2], strict=True)]
        return jnp.sum(jnp.sum(tiles[0], axis=1, keepdims=True), axis=0, keepdims=True)

    factor = values[...]
    residual = mttkrp[...] - operate(factor)
    direction, image = residual, operate(residual)
    now = inner(residual, residual)
    for step in range(ITERS):
        alpha = now / inner(direction, image)
        factor = factor + alpha * direction
        residual = residual - alpha * image
        if step < ITERS - 1:
            ahead, following = operate(residual), inner(residual, residual)
            beta = following / now
            direction = residual + beta * direction
            image = ahead + beta * image
            now = following
    start = pl.multiple_of(day * days, days)
    turn = jnp.where(stu == 0, 0, width - stu * columns)
    copies = []
    for i, (result, target) in enumerate(((factor, factor_hbm), (residual, residual_hbm))):
        block[i] = result
        rows = block[i, pl.ds(start, days), :]
        results[i] = pltpu.roll(rows, turn, axis=1)[:, :columns].T
        copies.append(pltpu.make_async_copy(results.at[i], target, sems.at[i]))
        copies[i].start()
    for copy in copies:
        copy.wait()


def conjugate(coef, prev, mine, other, gram, blocks, columns):
    days, width = prev.shape
    total = days * blocks
    shape = jax.ShapeDtypeStruct((columns, days), jnp.float32)
    return pl.pallas_call(
        functools.partial(cg_kernel, columns),
        compiler_params=pltpu.CompilerParams(vmem_limit_bytes=VMEM_BYTES),
        out_shape=(shape, shape),
        in_specs=[VMEM] * 5,
        out_specs=(HBM, HBM),
        scratch_shapes=[
            pltpu.VMEM((total, width), jnp.float32),
            pltpu.VMEM((total, width), jnp.float32),
            pltpu.VMEM((total + PAD, width), jnp.float32),
            pltpu.VMEM((total + PAD, width), jnp.float32),
            pltpu.VMEM((2, total, width), jnp.float32),
            pltpu.VMEM((2, columns, days), jnp.float32),
            pltpu.SemaphoreType.DMA((2,)),
        ],
        cost_estimate=pl.CostEstimate(
            flops=24 * total * width * width, bytes_accessed=4 * width * (width + 2 * total), transcendentals=0
        ),
    )(coef, prev, mine, other, gram)


def bits_of(count):
    assert count & (count - 1) == 0 and count > 1
    return [1 << b for b in range(count.bit_length() - 1)]


def local(performance, student_factor, skill_factor, day_prev, ar_coef):
    days = performance.shape[0]
    half = days // 2
    rank = skill_factor.shape[1]
    stu_size, day_size = lax.axis_size("stu"), lax.axis_size("day")
    send, skill, perf, student = send_part(performance, student_factor, skill_factor)
    got = exchange(send, 1)
    keep, day_prev, coef = keep_part(perf, skill, student, day_prev, ar_coef)
    skill_gram = lax.dot_general(skill, skill, (((0,), (0,)), ((), ())), preferred_element_type=jnp.float32)
    payload = jnp.concatenate([keep[:half] + got, keep[half:]], 0)
    masks = [bit | 1 for bit in bits_of(stu_size)[:0:-1]]
    for mask, other in zip(masks, masks[:-2] + masks[:-3:-1], strict=True):
        got = exchange(payload, mask, other)
        if mask == masks[0]:
            got, skill_gram = lax.optimization_barrier((got, skill_gram))
        payload = jnp.concatenate([payload[:half] + got[:half], payload[half:], got[half:]], 0)
    mttkrp, students = payload[:half], payload[half:]
    factor = lax.dynamic_slice_in_dim(day_prev, own_part() * half, half, 0)
    for bit in bits_of(day_size):
        got = exchange(jnp.concatenate([mttkrp, factor], 0), bit * stu_size + 1)
        rows = bit * half
        mttkrp = jnp.concatenate([mttkrp, got[:rows]], 0)
        factor = jnp.concatenate([factor, got[rows:]], 0)
    stack = gram_stack(students, exchange(students, 1), skill_gram)
    mine = jnp.concatenate([mttkrp, factor[half:]], 0)
    other = exchange(mine, 1)
    factor, residual = conjugate(coef, day_prev, mine, other, stack, day_size, rank // stu_size)
    return factor.T, residual.T


def solution(mesh):
    return jax.shard_map(
        local,
        mesh=mesh,
        in_specs=(P("day", "stu", None), P("stu", None), P(), P("day", None), P()),
        out_specs=(P("day", "stu"), P("day", "stu")),
        check_vma=False,
    )
```

```python
import functools

import jax
import jax.numpy as jnp
from jax import lax
from jax.experimental import pallas as pl
from jax.experimental.pallas import tpu as pltpu
from jax.sharding import PartitionSpec as P

LAGS = 7
ITERS = 3
PAD = 8
LANES = 128
VMEM_BYTES = 8 << 20


smoothing = 1.0

VMEM = pl.BlockSpec(memory_space=pltpu.VMEM)
HBM = pl.BlockSpec(memory_space=pltpu.HBM)


def exchange(block, mask, other=None):
    both = mask, mask if other is None else other
    union = both[0] | both[1]
    route = [(i, i ^ both[(i & union).bit_count() % 2]) for i in range(lax.axis_size(("day", "stu")))]
    return lax.ppermute(block, ("day", "stu"), route)


def own_part():
    place = lax.axis_index("day") ^ lax.axis_index("stu")
    for shift in (8, 4, 2, 1):
        place = place ^ (place >> shift)
    return place & 1


def split(values):
    high = values.astype(jnp.bfloat16)
    return high, (values - high.astype(jnp.float32)).astype(jnp.bfloat16)


def product(a, b):
    return jnp.dot(a, b, preferred_element_type=jnp.float32)


def student_sums(perf, skill, wide, proj, out_ref):
    students = wide.shape[0]
    total = product(perf[...], skill[...])
    days = total.shape[0] // students
    for t in range(proj.shape[0]):
        lanes = slice(t * LANES, (t + 1) * LANES)
        proj[t] = total[:, lanes]
        terms = None
        for s in range(students):
            row = proj[t, pl.ds(s, days, stride=students), :] * wide[s : s + 1, lanes]
            terms = row if terms is None else terms + row
        out_ref[:days, lanes] = terms


def send_kernel(perf_hbm, skill_hbm, student_hbm, send_ref, skill, keep, student, perf, proj, sems):
    rows = perf.shape[0]
    part = own_part()
    away = perf_hbm.at[pl.ds(pl.multiple_of((1 - part) * rows, rows), rows)]
    home = perf_hbm.at[pl.ds(pl.multiple_of(part * rows, rows), rows)]
    copies = []
    for i, (source, target) in enumerate(
        ((student_hbm, student), (skill_hbm, skill), (away, perf), (home, keep))
    ):
        copies.append(pltpu.make_async_copy(source, target, sems.at[i]))
        copies[i].start()
    for copy in copies[:3]:
        copy.wait()
    student_sums(perf, skill, student[...].astype(jnp.float32), proj, send_ref)
    copies[3].wait()


def send_part(performance, student_factor, skill_factor):
    days, students, skills = performance.shape
    rank = skill_factor.shape[1]
    rows = days * students // 2
    operands = performance.reshape(2 * rows, skills), skill_factor, student_factor
    return pl.pallas_call(
        send_kernel,
        compiler_params=pltpu.CompilerParams(vmem_limit_bytes=VMEM_BYTES),
        out_shape=(
            jax.ShapeDtypeStruct((days // 2, rank), jnp.float32),
            jax.ShapeDtypeStruct((skills, rank), jnp.bfloat16),
            jax.ShapeDtypeStruct((rows, skills), jnp.bfloat16),
            jax.ShapeDtypeStruct((students, rank), jnp.bfloat16),
        ),
        in_specs=[HBM] * 3,
        out_specs=(VMEM,) * 4,
        scratch_shapes=[
            pltpu.VMEM((rows, skills), jnp.bfloat16),
            pltpu.VMEM((rank // LANES, rows, LANES), jnp.float32),
            pltpu.SemaphoreType.DMA((4,)),
        ],
        cost_estimate=pl.CostEstimate(
            flops=2 * rows * skills * rank, bytes_accessed=2 * (2 * rows + rank) * skills, transcendentals=0
        ),
    )(*(pltpu.with_memory_space_constraint(x, pltpu.HBM) for x in operands))


def keep_kernel(perf, skill, student, prev_hbm, coef_hbm, keep_ref, prev, coef, proj, sems):
    copies = [
        pltpu.make_async_copy(prev_hbm, prev, sems.at[0]),
        pltpu.make_async_copy(coef_hbm, coef, sems.at[1]),
    ]
    for copy in copies:
        copy.start()
    wide = student[...].astype(jnp.float32)
    student_sums(perf, skill, wide, proj, keep_ref)
    keep_ref[-wide.shape[0] :, :] = wide
    for copy in copies:
        copy.wait()


def keep_part(perf, skill, student, prev, coef):
    rows, skills = perf.shape
    students, rank = student.shape
    small = prev, coef.reshape(1, LAGS)
    return pl.pallas_call(
        keep_kernel,
        compiler_params=pltpu.CompilerParams(vmem_limit_bytes=VMEM_BYTES),
        out_shape=(
            jax.ShapeDtypeStruct((rows // students + students, rank), jnp.float32),
            *(jax.ShapeDtypeStruct(x.shape, x.dtype) for x in small),
        ),
        in_specs=[VMEM] * 3 + [HBM] * 2,
        out_specs=(VMEM,) * 3,
        scratch_shapes=[
            pltpu.VMEM((rank // LANES, rows, LANES), jnp.float32),
            pltpu.SemaphoreType.DMA((2,)),
        ],
        cost_estimate=pl.CostEstimate(
            flops=2 * rows * skills * rank, bytes_accessed=2 * (rows + rank) * skills, transcendentals=0
        ),
    )(perf, skill, student, *(pltpu.with_memory_space_constraint(x, pltpu.HBM) for x in small))


def gram_kernel(mine_ref, other_ref, skill_gram_ref, out_ref):
    students = jnp.concatenate([mine_ref[...], other_ref[...]], 0).astype(jnp.bfloat16)
    student_gram = lax.dot_general(
        students, students, (((0,), (0,)), ((), ())), preferred_element_type=jnp.float32
    )
    rank = out_ref.shape[0]
    high, low = split(student_gram * skill_gram_ref[...])
    out_ref[:, :rank] = high
    out_ref[:, rank:] = low


def gram_stack(mine, other, skill_gram):
    count, rank = mine.shape
    return pl.pallas_call(
        gram_kernel,
        compiler_params=pltpu.CompilerParams(vmem_limit_bytes=VMEM_BYTES),
        out_shape=jax.ShapeDtypeStruct((rank, 2 * rank), jnp.bfloat16),
        in_specs=[VMEM] * 3,
        out_specs=VMEM,
        cost_estimate=pl.CostEstimate(
            flops=4 * count * rank * rank, bytes_accessed=8 * rank * rank, transcendentals=0
        ),
    )(mine, other, skill_gram)


def cg_kernel(
    columns, coef_ref, prev_ref, mine_ref, other_ref, gram_ref, factor_hbm, residual_hbm,
    mttkrp, values, low, high, block, results, sems,
):
    days, width = prev_ref.shape
    total = mttkrp.shape[0]
    blocks, half = total // days, days // 2
    day, stu, part = lax.axis_index("day"), lax.axis_index("stu"), own_part()
    values[pl.ds(pl.multiple_of(day * days, days), days), :] = prev_ref[...]
    for source, at in ((mine_ref, part), (other_ref, 1 - part)):
        for b in range(blocks):
            place = pl.ds(pl.multiple_of((day ^ b) * days + at * half, half), half)
            mttkrp[place, :] = source[b * half : (b + 1) * half, :]
            if b > 0:
                row = (blocks + b - 1) * half
                values[place, :] = source[row : row + half, :]
    gram_high, gram_wide = gram_ref[:, :width], gram_ref[...]
    low[:PAD, :] = jnp.zeros((PAD, width), jnp.float32)
    high[pl.ds(total, PAD), :] = jnp.zeros((PAD, width), jnp.float32)
    coef = [coef_ref[:, l : l + 1] for l in range(LAGS)]

    def operate(v):
        v_high, v_low = split(v)
        both = product(jnp.concatenate([v_high, v_low], 0), gram_wide)
        mixed = both[:total, :width] + (both[total:, :width] + both[:total, width:])
        low[pl.ds(PAD, total), :] = v
        ahead = v
        for lag in range(1, LAGS + 1):
            ahead = ahead - coef[lag - 1] * low[pl.ds(PAD - lag, total), :]
        high[:total, :] = ahead
        back = ahead
        for lag in range(1, LAGS + 1):
            back = back - coef[lag - 1] * high[pl.ds(lag, total), :]
        return mixed + smoothing * back

    def inner(a, b):
        terms = a * b
        tiles = [
            terms[i : i + PAD, j : j + LANES] for i in range(0, total, PAD) for j in range(0, width, LANES)
        ]
        while len(tiles) > 1:
            tiles = [x + y for x, y in zip(tiles[::2], tiles[1::2], strict=True)]
        return jnp.sum(jnp.sum(tiles[0], axis=1, keepdims=True), axis=0, keepdims=True)

    factor = values[...]
    residual = mttkrp[...] - operate(factor)
    start = pl.multiple_of(day * days, days)
    turn = jnp.where(stu == 0, 0, width - stu * columns)

    def own(v, slot):
        block[slot] = v
        return pltpu.roll(block[slot, pl.ds(start, days), :], turn, axis=1)[:, :columns].T

    direction, image = residual, operate(residual)
    now = inner(residual, residual)
    for step in range(ITERS - 1):
        alpha = now / inner(direction, image)
        factor = factor + alpha * direction
        residual = residual - alpha * image
        ahead, following = operate(residual), inner(residual, residual)
        beta = following / now
        direction = residual + beta * direction
        image = ahead + beta * image
        now = following
    alpha = now / inner(direction, image)
    results[0] = own(factor, 0) + alpha * own(direction, 1)
    results[1] = own(residual, 2) - alpha * own(image, 3)
    copies = []
    for i, target in enumerate((factor_hbm, residual_hbm)):
        copies.append(pltpu.make_async_copy(results.at[i], target, sems.at[i]))
        copies[i].start()
    for copy in copies:
        copy.wait()


def conjugate(coef, prev, mine, other, gram, blocks, columns):
    days, width = prev.shape
    total = days * blocks
    shape = jax.ShapeDtypeStruct((columns, days), jnp.float32)
    return pl.pallas_call(
        functools.partial(cg_kernel, columns),
        compiler_params=pltpu.CompilerParams(vmem_limit_bytes=VMEM_BYTES),
        out_shape=(shape, shape),
        in_specs=[VMEM] * 5,
        out_specs=(HBM, HBM),
        scratch_shapes=[
            pltpu.VMEM((total, width), jnp.float32),
            pltpu.VMEM((total, width), jnp.float32),
            pltpu.VMEM((total + PAD, width), jnp.float32),
            pltpu.VMEM((total + PAD, width), jnp.float32),
            pltpu.VMEM((4, total, width), jnp.float32),
            pltpu.VMEM((2, columns, days), jnp.float32),
            pltpu.SemaphoreType.DMA((2,)),
        ],
        cost_estimate=pl.CostEstimate(
            flops=24 * total * width * width, bytes_accessed=4 * width * (width + 2 * total), transcendentals=0
        ),
    )(coef, prev, mine, other, gram)


def bits_of(count):
    assert count & (count - 1) == 0 and count > 1
    return [1 << b for b in range(count.bit_length() - 1)]


def local(performance, student_factor, skill_factor, day_prev, ar_coef):
    days = performance.shape[0]
    half = days // 2
    rank = skill_factor.shape[1]
    stu_size, day_size = lax.axis_size("stu"), lax.axis_size("day")
    send, skill, perf, student = send_part(performance, student_factor, skill_factor)
    got = exchange(send, 1)
    keep, day_prev, coef = keep_part(perf, skill, student, day_prev, ar_coef)
    skill_gram = lax.dot_general(skill, skill, (((0,), (0,)), ((), ())), preferred_element_type=jnp.float32)
    payload = jnp.concatenate([keep[:half] + got, keep[half:]], 0)
    masks = [bit | 1 for bit in bits_of(stu_size)[:0:-1]]
    for mask, other in zip(masks, masks[:-2] + masks[:-3:-1], strict=True):
        got = exchange(payload, mask, other)
        if mask == masks[0]:
            got, skill_gram = lax.optimization_barrier((got, skill_gram))
        payload = jnp.concatenate([payload[:half] + got[:half], payload[half:], got[half:]], 0)
    mttkrp, students = payload[:half], payload[half:]
    factor = lax.dynamic_slice_in_dim(day_prev, own_part() * half, half, 0)
    for bit in bits_of(day_size):
        got = exchange(jnp.concatenate([mttkrp, factor], 0), bit * stu_size + 1)
        rows = bit * half
        mttkrp = jnp.concatenate([mttkrp, got[:rows]], 0)
        factor = jnp.concatenate([factor, got[rows:]], 0)
    stack = gram_stack(students, exchange(students, 1), skill_gram)
    mine = jnp.concatenate([mttkrp, factor[half:]], 0)
    other = exchange(mine, 1)
    factor, residual = conjugate(coef, day_prev, mine, other, stack, day_size, rank // stu_size)
    return factor.T, residual.T


def solution(mesh):
    return jax.shard_map(
        local,
        mesh=mesh,
        in_specs=(P("day", "stu", None), P("stu", None), P(), P("day", None), P()),
        out_specs=(P("day", "stu"), P("day", "stu")),
        check_vma=False,
    )
```

```python
import functools

import jax
import jax.numpy as jnp
from jax import lax
from jax.experimental import pallas as pl
from jax.experimental.pallas import tpu as pltpu
from jax.sharding import PartitionSpec as P

LAGS = 7
ITERS = 3
PAD = 8
LANES = 128
VMEM_BYTES = 8 << 20


smoothing = 1.0

VMEM = pl.BlockSpec(memory_space=pltpu.VMEM)
HBM = pl.BlockSpec(memory_space=pltpu.HBM)


def exchange(block, mask, other=None):
    both = mask, mask if other is None else other
    union = both[0] | both[1]
    route = [(i, i ^ both[(i & union).bit_count() % 2]) for i in range(lax.axis_size(("day", "stu")))]
    return lax.ppermute(block, ("day", "stu"), route)


def own_part():
    place = lax.axis_index("day") ^ lax.axis_index("stu")
    for shift in (8, 4, 2, 1):
        place = place ^ (place >> shift)
    return place & 1


def split(values):
    high = values.astype(jnp.bfloat16)
    return high, (values - high.astype(jnp.float32)).astype(jnp.bfloat16)


def product(a, b):
    return jnp.dot(a, b, preferred_element_type=jnp.float32)


def student_sums(perf, skill, wide, proj, out_ref):
    students = wide.shape[0]
    total = product(perf[...], skill[...])
    days = total.shape[0] // students
    for t in range(proj.shape[0]):
        lanes = slice(t * LANES, (t + 1) * LANES)
        proj[t] = total[:, lanes]
        terms = None
        for s in range(students):
            row = proj[t, pl.ds(s, days, stride=students), :] * wide[s : s + 1, lanes]
            terms = row if terms is None else terms + row
        out_ref[:days, lanes] = terms


def send_kernel(perf_hbm, skill_hbm, student_hbm, send_ref, skill, keep, student, perf, proj, sems):
    rows = perf.shape[0]
    part = own_part()
    away = perf_hbm.at[pl.ds(pl.multiple_of((1 - part) * rows, rows), rows)]
    home = perf_hbm.at[pl.ds(pl.multiple_of(part * rows, rows), rows)]
    copies = []
    for i, (source, target) in enumerate(
        ((student_hbm, student), (skill_hbm, skill), (away, perf), (home, keep))
    ):
        copies.append(pltpu.make_async_copy(source, target, sems.at[i]))
        copies[i].start()
    for copy in copies[:3]:
        copy.wait()
    student_sums(perf, skill, student[...].astype(jnp.float32), proj, send_ref)
    copies[3].wait()


def send_part(performance, student_factor, skill_factor):
    days, students, skills = performance.shape
    rank = skill_factor.shape[1]
    rows = days * students // 2
    operands = performance.reshape(2 * rows, skills), skill_factor, student_factor
    return pl.pallas_call(
        send_kernel,
        compiler_params=pltpu.CompilerParams(vmem_limit_bytes=VMEM_BYTES),
        out_shape=(
            jax.ShapeDtypeStruct((days // 2, rank), jnp.float32),
            jax.ShapeDtypeStruct((skills, rank), jnp.bfloat16),
            jax.ShapeDtypeStruct((rows, skills), jnp.bfloat16),
            jax.ShapeDtypeStruct((students, rank), jnp.bfloat16),
        ),
        in_specs=[HBM] * 3,
        out_specs=(VMEM,) * 4,
        scratch_shapes=[
            pltpu.VMEM((rows, skills), jnp.bfloat16),
            pltpu.VMEM((rank // LANES, rows, LANES), jnp.float32),
            pltpu.SemaphoreType.DMA((4,)),
        ],
        cost_estimate=pl.CostEstimate(
            flops=2 * rows * skills * rank, bytes_accessed=2 * (2 * rows + rank) * skills, transcendentals=0
        ),
    )(*(pltpu.with_memory_space_constraint(x, pltpu.HBM) for x in operands))


def keep_kernel(perf, skill, student, prev_hbm, coef_hbm, keep_ref, prev, coef, proj, sems):
    copies = [
        pltpu.make_async_copy(prev_hbm, prev, sems.at[0]),
        pltpu.make_async_copy(coef_hbm, coef, sems.at[1]),
    ]
    for copy in copies:
        copy.start()
    wide = student[...].astype(jnp.float32)
    student_sums(perf, skill, wide, proj, keep_ref)
    keep_ref[-wide.shape[0] :, :] = wide
    for copy in copies:
        copy.wait()


def keep_part(perf, skill, student, prev, coef):
    rows, skills = perf.shape
    students, rank = student.shape
    small = prev, coef.reshape(1, LAGS)
    return pl.pallas_call(
        keep_kernel,
        compiler_params=pltpu.CompilerParams(vmem_limit_bytes=VMEM_BYTES),
        out_shape=(
            jax.ShapeDtypeStruct((rows // students + students, rank), jnp.float32),
            *(jax.ShapeDtypeStruct(x.shape, x.dtype) for x in small),
        ),
        in_specs=[VMEM] * 3 + [HBM] * 2,
        out_specs=(VMEM,) * 3,
        scratch_shapes=[
            pltpu.VMEM((rank // LANES, rows, LANES), jnp.float32),
            pltpu.SemaphoreType.DMA((2,)),
        ],
        cost_estimate=pl.CostEstimate(
            flops=2 * rows * skills * rank, bytes_accessed=2 * (rows + rank) * skills, transcendentals=0
        ),
    )(perf, skill, student, *(pltpu.with_memory_space_constraint(x, pltpu.HBM) for x in small))


def gram_kernel(mine_ref, other_ref, skill_gram_ref, out_ref):
    students = jnp.concatenate([mine_ref[...], other_ref[...]], 0).astype(jnp.bfloat16)
    student_gram = lax.dot_general(
        students, students, (((0,), (0,)), ((), ())), preferred_element_type=jnp.float32
    )
    rank = out_ref.shape[0]
    high, low = split(student_gram * skill_gram_ref[...])
    out_ref[:, :rank] = high
    out_ref[:, rank:] = low


def gram_stack(mine, other, skill_gram):
    count, rank = mine.shape
    return pl.pallas_call(
        gram_kernel,
        compiler_params=pltpu.CompilerParams(vmem_limit_bytes=VMEM_BYTES),
        out_shape=jax.ShapeDtypeStruct((rank, 2 * rank), jnp.bfloat16),
        in_specs=[VMEM] * 3,
        out_specs=VMEM,
        cost_estimate=pl.CostEstimate(
            flops=4 * count * rank * rank, bytes_accessed=8 * rank * rank, transcendentals=0
        ),
    )(mine, other, skill_gram)


def cg_kernel(
    columns, coef_ref, prev_ref, mine_ref, other_ref, gram_ref, factor_hbm, residual_hbm,
    mttkrp, values, block, results, sems,
):
    days, width = prev_ref.shape
    total = mttkrp.shape[0]
    blocks, half = total // days, days // 2
    day, stu, part = lax.axis_index("day"), lax.axis_index("stu"), own_part()
    values[pl.ds(pl.multiple_of(day * days, days), days), :] = prev_ref[...]
    for source, at in ((mine_ref, part), (other_ref, 1 - part)):
        for b in range(blocks):
            place = pl.ds(pl.multiple_of((day ^ b) * days + at * half, half), half)
            mttkrp[place, :] = source[b * half : (b + 1) * half, :]
            if b > 0:
                row = (blocks + b - 1) * half
                values[place, :] = source[row : row + half, :]
    gram_high, gram_wide = gram_ref[:, :width], gram_ref[...]
    blank = jnp.zeros((PAD, LANES), jnp.float32)
    coef = [coef_ref[:, l : l + 1] for l in range(LAGS)]

    def operate(v):
        v_high, v_low = split(v)
        both = product(jnp.concatenate([v_high, v_low], 0), gram_wide)
        mixed = both[:total, :width] + (both[total:, :width] + both[:total, width:])
        back = jnp.concatenate([smooth(v[:, t : t + LANES]) for t in range(0, width, LANES)], 1)
        return mixed + smoothing * back

    def smooth(v):
        padded = jnp.concatenate([blank, v], 0)
        ahead = v
        for lag in range(1, LAGS + 1):
            ahead = ahead - coef[lag - 1] * pltpu.roll(padded, lag, axis=0)[PAD:]
        padded = jnp.concatenate([ahead, blank], 0)
        back = ahead
        for lag in range(1, LAGS + 1):
            back = back - coef[lag - 1] * pltpu.roll(padded, total + PAD - lag, axis=0)[:total]
        return back

    def inner(a, b):
        terms = a * b
        tiles = [
            terms[i : i + PAD, j : j + LANES] for i in range(0, total, PAD) for j in range(0, width, LANES)
        ]
        while len(tiles) > 1:
            tiles = [x + y for x, y in zip(tiles[::2], tiles[1::2], strict=True)]
        return jnp.sum(jnp.sum(tiles[0], axis=1, keepdims=True), axis=0, keepdims=True)

    factor = values[...]
    residual = mttkrp[...] - operate(factor)
    start = pl.multiple_of(day * days, days)
    turn = jnp.where(stu == 0, 0, width - stu * columns)

    def own(v, slot):
        block[slot] = v
        return pltpu.roll(block[slot, pl.ds(start, days), :], turn, axis=1)[:, :columns].T

    direction, image = residual, operate(residual)
    now = inner(residual, residual)
    for step in range(ITERS - 1):
        alpha = now / inner(direction, image)
        factor = factor + alpha * direction
        residual = residual - alpha * image
        ahead, following = operate(residual), inner(residual, residual)
        beta = following / now
        direction = residual + beta * direction
        image = ahead + beta * image
        now = following
    alpha = now / inner(direction, image)
    results[0] = own(factor, 0) + alpha * own(direction, 1)
    results[1] = own(residual, 2) - alpha * own(image, 3)
    copies = []
    for i, target in enumerate((factor_hbm, residual_hbm)):
        copies.append(pltpu.make_async_copy(results.at[i], target, sems.at[i]))
        copies[i].start()
    for copy in copies:
        copy.wait()


def conjugate(coef, prev, mine, other, gram, blocks, columns):
    days, width = prev.shape
    total = days * blocks
    shape = jax.ShapeDtypeStruct((columns, days), jnp.float32)
    return pl.pallas_call(
        functools.partial(cg_kernel, columns),
        compiler_params=pltpu.CompilerParams(vmem_limit_bytes=VMEM_BYTES),
        out_shape=(shape, shape),
        in_specs=[VMEM] * 5,
        out_specs=(HBM, HBM),
        scratch_shapes=[
            pltpu.VMEM((total, width), jnp.float32),
            pltpu.VMEM((total, width), jnp.float32),
            pltpu.VMEM((4, total, width), jnp.float32),
            pltpu.VMEM((2, columns, days), jnp.float32),
            pltpu.SemaphoreType.DMA((2,)),
        ],
        cost_estimate=pl.CostEstimate(
            flops=24 * total * width * width, bytes_accessed=4 * width * (width + 2 * total), transcendentals=0
        ),
    )(coef, prev, mine, other, gram)


def bits_of(count):
    assert count & (count - 1) == 0 and count > 1
    return [1 << b for b in range(count.bit_length() - 1)]


def local(performance, student_factor, skill_factor, day_prev, ar_coef):
    days = performance.shape[0]
    half = days // 2
    rank = skill_factor.shape[1]
    stu_size, day_size = lax.axis_size("stu"), lax.axis_size("day")
    send, skill, perf, student = send_part(performance, student_factor, skill_factor)
    got = exchange(send, 1)
    keep, day_prev, coef = keep_part(perf, skill, student, day_prev, ar_coef)
    skill_gram = lax.dot_general(skill, skill, (((0,), (0,)), ((), ())), preferred_element_type=jnp.float32)
    payload = jnp.concatenate([keep[:half] + got, keep[half:]], 0)
    masks = [bit | 1 for bit in bits_of(stu_size)[:0:-1]]
    for mask, other in zip(masks, masks[:-2] + masks[:-3:-1], strict=True):
        got = exchange(payload, mask, other)
        if mask == masks[0]:
            got, skill_gram = lax.optimization_barrier((got, skill_gram))
        payload = jnp.concatenate([payload[:half] + got[:half], payload[half:], got[half:]], 0)
    mttkrp, students = payload[:half], payload[half:]
    factor = lax.dynamic_slice_in_dim(day_prev, own_part() * half, half, 0)
    for bit in bits_of(day_size):
        got = exchange(jnp.concatenate([mttkrp, factor], 0), bit * stu_size + 1)
        rows = bit * half
        mttkrp = jnp.concatenate([mttkrp, got[:rows]], 0)
        factor = jnp.concatenate([factor, got[rows:]], 0)
    stack = gram_stack(students, exchange(students, 1), skill_gram)
    mine = jnp.concatenate([mttkrp, factor[half:]], 0)
    other = exchange(mine, 1)
    factor, residual = conjugate(coef, day_prev, mine, other, stack, day_size, rank // stu_size)
    return factor.T, residual.T


def solution(mesh):
    return jax.shard_map(
        local,
        mesh=mesh,
        in_specs=(P("day", "stu", None), P("stu", None), P(), P("day", None), P()),
        out_specs=(P("day", "stu"), P("day", "stu")),
        check_vma=False,
    )
```

```python
import functools

import jax
import jax.numpy as jnp
from jax import lax
from jax.experimental import pallas as pl
from jax.experimental.pallas import tpu as pltpu
from jax.sharding import PartitionSpec as P

LAGS = 7
ITERS = 3
PAD = 8
LANES = 128
VMEM_BYTES = 8 << 20


smoothing = 1.0

VMEM = pl.BlockSpec(memory_space=pltpu.VMEM)
HBM = pl.BlockSpec(memory_space=pltpu.HBM)


def exchange(block, mask, other=None):
    both = mask, mask if other is None else other
    union = both[0] | both[1]
    route = [(i, i ^ both[(i & union).bit_count() % 2]) for i in range(lax.axis_size(("day", "stu")))]
    return lax.ppermute(block, ("day", "stu"), route)


def own_part():
    place = lax.axis_index("day") ^ lax.axis_index("stu")
    for shift in (8, 4, 2, 1):
        place = place ^ (place >> shift)
    return place & 1


def split(values):
    high = values.astype(jnp.bfloat16)
    return high, (values - high.astype(jnp.float32)).astype(jnp.bfloat16)


def product(a, b):
    return jnp.dot(a, b, preferred_element_type=jnp.float32)


def student_sums(perf, skill, wide, proj, out_ref):
    students = wide.shape[0]
    total = product(perf[...], skill[...])
    days = total.shape[0] // students
    for t in range(proj.shape[0]):
        lanes = slice(t * LANES, (t + 1) * LANES)
        proj[t, : total.shape[0], :] = total[:, lanes]
        terms = None
        for s in range(students):
            row = proj[t, pl.ds(s, days, stride=students), :] * wide[s : s + 1, lanes]
            terms = row if terms is None else terms + row
        out_ref[:days, lanes] = terms


def send_kernel(perf_hbm, skill_hbm, student_hbm, send_ref, skill, keep, student, perf, proj, sems):
    rows = perf.shape[0]
    part = own_part()
    away = perf_hbm.at[pl.ds(pl.multiple_of((1 - part) * rows, rows), rows)]
    home = perf_hbm.at[pl.ds(pl.multiple_of(part * rows, rows), rows)]
    copies = []
    for i, (source, target) in enumerate(
        ((student_hbm, student), (skill_hbm, skill), (away, perf), (home, keep))
    ):
        copies.append(pltpu.make_async_copy(source, target, sems.at[i]))
        copies[i].start()
    for copy in copies[:3]:
        copy.wait()
    student_sums(perf, skill, student[...].astype(jnp.float32), proj, send_ref)
    copies[3].wait()


def send_part(performance, student_factor, skill_factor):
    days, students, skills = performance.shape
    rank = skill_factor.shape[1]
    rows = days * students // 2
    operands = performance.reshape(2 * rows, skills), skill_factor, student_factor
    return pl.pallas_call(
        send_kernel,
        compiler_params=pltpu.CompilerParams(vmem_limit_bytes=VMEM_BYTES),
        out_shape=(
            jax.ShapeDtypeStruct((days // 2, rank), jnp.float32),
            jax.ShapeDtypeStruct((skills, rank), jnp.bfloat16),
            jax.ShapeDtypeStruct((rows, skills), jnp.bfloat16),
            jax.ShapeDtypeStruct((students, rank), jnp.bfloat16),
        ),
        in_specs=[HBM] * 3,
        out_specs=(VMEM,) * 4,
        scratch_shapes=[
            pltpu.VMEM((rows, skills), jnp.bfloat16),
            pltpu.VMEM((rank // LANES, rows + students, LANES), jnp.float32),
            pltpu.SemaphoreType.DMA((4,)),
        ],
        cost_estimate=pl.CostEstimate(
            flops=2 * rows * skills * rank, bytes_accessed=2 * (2 * rows + rank) * skills, transcendentals=0
        ),
    )(*(pltpu.with_memory_space_constraint(x, pltpu.HBM) for x in operands))


def keep_kernel(perf, skill, student, prev_hbm, coef_hbm, keep_ref, prev, coef, proj, sems):
    copies = [
        pltpu.make_async_copy(prev_hbm, prev, sems.at[0]),
        pltpu.make_async_copy(coef_hbm, coef, sems.at[1]),
    ]
    for copy in copies:
        copy.start()
    wide = student[...].astype(jnp.float32)
    student_sums(perf, skill, wide, proj, keep_ref)
    keep_ref[-wide.shape[0] :, :] = wide
    for copy in copies:
        copy.wait()


def keep_part(perf, skill, student, prev, coef):
    rows, skills = perf.shape
    students, rank = student.shape
    small = prev, coef.reshape(1, LAGS)
    return pl.pallas_call(
        keep_kernel,
        compiler_params=pltpu.CompilerParams(vmem_limit_bytes=VMEM_BYTES),
        out_shape=(
            jax.ShapeDtypeStruct((rows // students + students, rank), jnp.float32),
            *(jax.ShapeDtypeStruct(x.shape, x.dtype) for x in small),
        ),
        in_specs=[VMEM] * 3 + [HBM] * 2,
        out_specs=(VMEM,) * 3,
        scratch_shapes=[
            pltpu.VMEM((rank // LANES, rows + students, LANES), jnp.float32),
            pltpu.SemaphoreType.DMA((2,)),
        ],
        cost_estimate=pl.CostEstimate(
            flops=2 * rows * skills * rank, bytes_accessed=2 * (rows + rank) * skills, transcendentals=0
        ),
    )(perf, skill, student, *(pltpu.with_memory_space_constraint(x, pltpu.HBM) for x in small))


def gram_kernel(mine_ref, other_ref, skill_gram_ref, out_ref):
    students = jnp.concatenate([mine_ref[...], other_ref[...]], 0).astype(jnp.bfloat16)
    student_gram = lax.dot_general(
        students, students, (((0,), (0,)), ((), ())), preferred_element_type=jnp.float32
    )
    rank = out_ref.shape[0]
    high, low = split(student_gram * skill_gram_ref[...])
    out_ref[:, :rank] = high
    out_ref[:, rank:] = low


def gram_stack(mine, other, skill_gram):
    count, rank = mine.shape
    return pl.pallas_call(
        gram_kernel,
        compiler_params=pltpu.CompilerParams(vmem_limit_bytes=VMEM_BYTES),
        out_shape=jax.ShapeDtypeStruct((rank, 2 * rank), jnp.bfloat16),
        in_specs=[VMEM] * 3,
        out_specs=VMEM,
        cost_estimate=pl.CostEstimate(
            flops=4 * count * rank * rank, bytes_accessed=8 * rank * rank, transcendentals=0
        ),
    )(mine, other, skill_gram)


def cg_kernel(
    columns, coef_ref, prev_ref, mine_ref, other_ref, gram_ref, factor_hbm, residual_hbm,
    mttkrp, values, block, results, sems,
):
    days, width = prev_ref.shape
    total = mttkrp.shape[0]
    blocks, half = total // days, days // 2
    day, stu, part = lax.axis_index("day"), lax.axis_index("stu"), own_part()
    values[pl.ds(pl.multiple_of(day * days, days), days), :] = prev_ref[...]
    for source, at in ((mine_ref, part), (other_ref, 1 - part)):
        for b in range(blocks):
            place = pl.ds(pl.multiple_of((day ^ b) * days + at * half, half), half)
            mttkrp[place, :] = source[b * half : (b + 1) * half, :]
            if b > 0:
                row = (blocks + b - 1) * half
                values[place, :] = source[row : row + half, :]
    gram_high, gram_wide = gram_ref[:, :width], gram_ref[...]
    blank = jnp.zeros((PAD, LANES), jnp.float32)
    coef = [coef_ref[:, l : l + 1] for l in range(LAGS)]

    def operate(v):
        v_high, v_low = split(v)
        both = product(jnp.concatenate([v_high, v_low], 0), gram_wide)
        mixed = both[:total, :width] + (both[total:, :width] + both[:total, width:])
        back = jnp.concatenate([smooth(v[:, t : t + LANES]) for t in range(0, width, LANES)], 1)
        return mixed + smoothing * back

    def smooth(v):
        padded = jnp.concatenate([blank, v], 0)
        ahead = v
        for lag in range(1, LAGS + 1):
            ahead = ahead - coef[lag - 1] * pltpu.roll(padded, lag, axis=0)[PAD:]
        padded = jnp.concatenate([ahead, blank], 0)
        back = ahead
        for lag in range(1, LAGS + 1):
            back = back - coef[lag - 1] * pltpu.roll(padded, total + PAD - lag, axis=0)[:total]
        return back

    def inner(a, b):
        terms = a * b
        tiles = [
            terms[i : i + PAD, j : j + LANES] for i in range(0, total, PAD) for j in range(0, width, LANES)
        ]
        while len(tiles) > 1:
            tiles = [x + y for x, y in zip(tiles[::2], tiles[1::2], strict=True)]
        return jnp.sum(jnp.sum(tiles[0], axis=1, keepdims=True), axis=0, keepdims=True)

    factor = values[...]
    residual = mttkrp[...] - operate(factor)
    start = pl.multiple_of(day * days, days)
    turn = jnp.where(stu == 0, 0, width - stu * columns)

    def own(v, slot):
        block[slot] = v
        return pltpu.roll(block[slot, pl.ds(start, days), :], turn, axis=1)[:, :columns].T

    direction, image = residual, operate(residual)
    now = inner(residual, residual)
    for step in range(ITERS - 1):
        alpha = now / inner(direction, image)
        factor = factor + alpha * direction
        residual = residual - alpha * image
        ahead, following = operate(residual), inner(residual, residual)
        beta = following / now
        direction = residual + beta * direction
        image = ahead + beta * image
        now = following
    alpha = now / inner(direction, image)
    results[0] = own(factor, 0) + alpha * own(direction, 1)
    results[1] = own(residual, 2) - alpha * own(image, 3)
    copies = []
    for i, target in enumerate((factor_hbm, residual_hbm)):
        copies.append(pltpu.make_async_copy(results.at[i], target, sems.at[i]))
        copies[i].start()
    for copy in copies:
        copy.wait()


def conjugate(coef, prev, mine, other, gram, blocks, columns):
    days, width = prev.shape
    total = days * blocks
    shape = jax.ShapeDtypeStruct((columns, days), jnp.float32)
    return pl.pallas_call(
        functools.partial(cg_kernel, columns),
        compiler_params=pltpu.CompilerParams(vmem_limit_bytes=VMEM_BYTES),
        out_shape=(shape, shape),
        in_specs=[VMEM] * 5,
        out_specs=(HBM, HBM),
        scratch_shapes=[
            pltpu.VMEM((total, width), jnp.float32),
            pltpu.VMEM((total, width), jnp.float32),
            pltpu.VMEM((4, total, width), jnp.float32),
            pltpu.VMEM((2, columns, days), jnp.float32),
            pltpu.SemaphoreType.DMA((2,)),
        ],
        cost_estimate=pl.CostEstimate(
            flops=24 * total * width * width, bytes_accessed=4 * width * (width + 2 * total), transcendentals=0
        ),
    )(coef, prev, mine, other, gram)


def bits_of(count):
    assert count & (count - 1) == 0 and count > 1
    return [1 << b for b in range(count.bit_length() - 1)]


def local(performance, student_factor, skill_factor, day_prev, ar_coef):
    days = performance.shape[0]
    half = days // 2
    rank = skill_factor.shape[1]
    stu_size, day_size = lax.axis_size("stu"), lax.axis_size("day")
    send, skill, perf, student = send_part(performance, student_factor, skill_factor)
    got = exchange(send, 1)
    keep, day_prev, coef = keep_part(perf, skill, student, day_prev, ar_coef)
    skill_gram = lax.dot_general(skill, skill, (((0,), (0,)), ((), ())), preferred_element_type=jnp.float32)
    payload = jnp.concatenate([keep[:half] + got, keep[half:]], 0)
    masks = [bit | 1 for bit in bits_of(stu_size)[:0:-1]]
    for mask, other in zip(masks, masks[:-2] + masks[:-3:-1], strict=True):
        got = exchange(payload, mask, other)
        if mask == masks[0]:
            got, skill_gram = lax.optimization_barrier((got, skill_gram))
        payload = jnp.concatenate([payload[:half] + got[:half], payload[half:], got[half:]], 0)
    mttkrp, students = payload[:half], payload[half:]
    factor = lax.dynamic_slice_in_dim(day_prev, own_part() * half, half, 0)
    for bit in bits_of(day_size):
        got = exchange(jnp.concatenate([mttkrp, factor], 0), bit * stu_size + 1)
        rows = bit * half
        mttkrp = jnp.concatenate([mttkrp, got[:rows]], 0)
        factor = jnp.concatenate([factor, got[rows:]], 0)
    stack = gram_stack(students, exchange(students, 1), skill_gram)
    mine = jnp.concatenate([mttkrp, factor[half:]], 0)
    other = exchange(mine, 1)
    factor, residual = conjugate(coef, day_prev, mine, other, stack, day_size, rank // stu_size)
    return factor.T, residual.T


def solution(mesh):
    return jax.shard_map(
        local,
        mesh=mesh,
        in_specs=(P("day", "stu", None), P("stu", None), P(), P("day", None), P()),
        out_specs=(P("day", "stu"), P("day", "stu")),
        check_vma=False,
    )
```

```python
import functools

import jax
import jax.numpy as jnp
from jax import lax
from jax.experimental import pallas as pl
from jax.experimental.pallas import tpu as pltpu
from jax.sharding import PartitionSpec as P

LAGS = 7
ITERS = 3
PAD = 8
LANES = 128
VMEM_BYTES = 8 << 20


smoothing = 1.0

VMEM = pl.BlockSpec(memory_space=pltpu.VMEM)
HBM = pl.BlockSpec(memory_space=pltpu.HBM)


def exchange(block, mask, other=None):
    both = mask, mask if other is None else other
    union = both[0] | both[1]
    route = [(i, i ^ both[(i & union).bit_count() % 2]) for i in range(lax.axis_size(("day", "stu")))]
    return lax.ppermute(block, ("day", "stu"), route)


def own_part():
    place = lax.axis_index("day") ^ lax.axis_index("stu")
    for shift in (8, 4, 2, 1):
        place = place ^ (place >> shift)
    return place & 1


def split(values):
    high = values.astype(jnp.bfloat16)
    return high, (values - high.astype(jnp.float32)).astype(jnp.bfloat16)


def product(a, b):
    return jnp.dot(a, b, preferred_element_type=jnp.float32)


def student_sums(perf, skill, wide, proj, out_ref):
    students = wide.shape[0]
    total = product(perf[...], skill[...])
    days = total.shape[0] // students
    for t in range(proj.shape[0]):
        lanes = slice(t * LANES, (t + 1) * LANES)
        proj[t, : total.shape[0], :] = total[:, lanes]
        terms = None
        for s in range(students):
            row = proj[t, pl.ds(s, days, stride=students), :] * wide[s : s + 1, lanes]
            terms = row if terms is None else terms + row
        out_ref[:days, lanes] = terms


def send_kernel(perf_hbm, skill_hbm, student_hbm, send_ref, skill, keep, student, perf, proj, sems):
    rows = perf.shape[0]
    part = own_part()
    away = perf_hbm.at[pl.ds(pl.multiple_of((1 - part) * rows, rows), rows)]
    home = perf_hbm.at[pl.ds(pl.multiple_of(part * rows, rows), rows)]
    copies = []
    for i, (source, target) in enumerate(
        ((student_hbm, student), (skill_hbm, skill), (away, perf), (home, keep))
    ):
        copies.append(pltpu.make_async_copy(source, target, sems.at[i]))
        copies[i].start()
    for copy in copies[:3]:
        copy.wait()
    student_sums(perf, skill, student[...].astype(jnp.float32), proj, send_ref)
    copies[3].wait()


def send_part(performance, student_factor, skill_factor):
    days, students, skills = performance.shape
    rank = skill_factor.shape[1]
    rows = days * students // 2
    operands = performance.reshape(2 * rows, skills), skill_factor, student_factor
    return pl.pallas_call(
        send_kernel,
        compiler_params=pltpu.CompilerParams(vmem_limit_bytes=VMEM_BYTES),
        out_shape=(
            jax.ShapeDtypeStruct((days // 2, rank), jnp.float32),
            jax.ShapeDtypeStruct((skills, rank), jnp.bfloat16),
            jax.ShapeDtypeStruct((rows, skills), jnp.bfloat16),
            jax.ShapeDtypeStruct((students, rank), jnp.bfloat16),
        ),
        in_specs=[HBM] * 3,
        out_specs=(VMEM,) * 4,
        scratch_shapes=[
            pltpu.VMEM((rows, skills), jnp.bfloat16),
            pltpu.VMEM((rank // LANES, rows + students, LANES), jnp.float32),
            pltpu.SemaphoreType.DMA((4,)),
        ],
        cost_estimate=pl.CostEstimate(
            flops=2 * rows * skills * rank, bytes_accessed=2 * (2 * rows + rank) * skills, transcendentals=0
        ),
    )(*(pltpu.with_memory_space_constraint(x, pltpu.HBM) for x in operands))


def keep_kernel(perf, skill, student, prev_hbm, coef_hbm, keep_ref, prev, coef, proj, sems):
    copies = [
        pltpu.make_async_copy(prev_hbm, prev, sems.at[0]),
        pltpu.make_async_copy(coef_hbm, coef, sems.at[1]),
    ]
    for copy in copies:
        copy.start()
    wide = student[...].astype(jnp.float32)
    student_sums(perf, skill, wide, proj, keep_ref)
    keep_ref[-wide.shape[0] :, :] = wide
    for copy in copies:
        copy.wait()


def keep_part(perf, skill, student, prev, coef):
    rows, skills = perf.shape
    students, rank = student.shape
    small = prev, coef.reshape(1, LAGS)
    return pl.pallas_call(
        keep_kernel,
        compiler_params=pltpu.CompilerParams(vmem_limit_bytes=VMEM_BYTES),
        out_shape=(
            jax.ShapeDtypeStruct((rows // students + students, rank), jnp.float32),
            *(jax.ShapeDtypeStruct(x.shape, x.dtype) for x in small),
        ),
        in_specs=[VMEM] * 3 + [HBM] * 2,
        out_specs=(VMEM,) * 3,
        scratch_shapes=[
            pltpu.VMEM((rank // LANES, rows + students, LANES), jnp.float32),
            pltpu.SemaphoreType.DMA((2,)),
        ],
        cost_estimate=pl.CostEstimate(
            flops=2 * rows * skills * rank, bytes_accessed=2 * (rows + rank) * skills, transcendentals=0
        ),
    )(perf, skill, student, *(pltpu.with_memory_space_constraint(x, pltpu.HBM) for x in small))


def gram_kernel(first, mine_ref, early_ref, late_ref, skill_gram_ref, out_ref):
    students = jnp.concatenate([mine_ref[...], early_ref[...], late_ref[first:, :]], 0).astype(jnp.bfloat16)
    student_gram = lax.dot_general(
        students, students, (((0,), (0,)), ((), ())), preferred_element_type=jnp.float32
    )
    rank = out_ref.shape[0]
    high, low = split(student_gram * skill_gram_ref[...])
    out_ref[:, :rank] = high
    out_ref[:, rank:] = low


def gram_stack(first, mine, early, late, skill_gram):
    count, rank = mine.shape
    return pl.pallas_call(
        functools.partial(gram_kernel, first),
        compiler_params=pltpu.CompilerParams(vmem_limit_bytes=VMEM_BYTES),
        out_shape=jax.ShapeDtypeStruct((rank, 2 * rank), jnp.bfloat16),
        in_specs=[VMEM] * 4,
        out_specs=VMEM,
        cost_estimate=pl.CostEstimate(
            flops=4 * count * rank * rank, bytes_accessed=8 * rank * rank, transcendentals=0
        ),
    )(mine, early, late, skill_gram)


def cg_kernel(
    columns, coef_ref, prev_ref, mine_ref, core_ref, far_ref, cross_ref, gram_ref, factor_hbm, residual_hbm,
    mttkrp, values, block, results, sems,
):
    days, width = prev_ref.shape
    total = mttkrp.shape[0]
    near, half = total // days // 2, days // 2
    day, stu, part = lax.axis_index("day"), lax.axis_index("stu"), own_part()
    values[pl.ds(pl.multiple_of(day * days, days), days), :] = prev_ref[...]
    for at, near_ref, away_ref in ((part, mine_ref, far_ref), (1 - part, core_ref, cross_ref)):
        for b in range(2 * near):
            source, row, step = (near_ref, b, near - 1) if b < near else (away_ref, b - near, near)
            place = pl.ds(pl.multiple_of((day ^ b) * days + at * half, half), half)
            mttkrp[place, :] = source[row * half : (row + 1) * half, :]
            if b > 0:
                values[place, :] = source[(row + step) * half : (row + step + 1) * half, :]
    gram_high, gram_wide = gram_ref[:, :width], gram_ref[...]
    blank = jnp.zeros((PAD, LANES), jnp.float32)
    coef = [coef_ref[:, l : l + 1] for l in range(LAGS)]

    def operate(v):
        v_high, v_low = split(v)
        both = product(jnp.concatenate([v_high, v_low], 0), gram_wide)
        mixed = both[:total, :width] + (both[total:, :width] + both[:total, width:])
        back = jnp.concatenate([smooth(v[:, t : t + LANES]) for t in range(0, width, LANES)], 1)
        return mixed + smoothing * back

    def smooth(v):
        padded = jnp.concatenate([blank, v], 0)
        ahead = v
        for lag in range(1, LAGS + 1):
            ahead = ahead - coef[lag - 1] * pltpu.roll(padded, lag, axis=0)[PAD:]
        padded = jnp.concatenate([ahead, blank], 0)
        back = ahead
        for lag in range(1, LAGS + 1):
            back = back - coef[lag - 1] * pltpu.roll(padded, total + PAD - lag, axis=0)[:total]
        return back

    def inner(a, b):
        terms = a * b
        tiles = [
            terms[i : i + PAD, j : j + LANES] for i in range(0, total, PAD) for j in range(0, width, LANES)
        ]
        while len(tiles) > 1:
            tiles = [x + y for x, y in zip(tiles[::2], tiles[1::2], strict=True)]
        return jnp.sum(jnp.sum(tiles[0], axis=1, keepdims=True), axis=0, keepdims=True)

    factor = values[...]
    residual = mttkrp[...] - operate(factor)
    start = pl.multiple_of(day * days, days)
    turn = jnp.where(stu == 0, 0, width - stu * columns)

    def own(v, slot):
        block[slot] = v
        return pltpu.roll(block[slot, pl.ds(start, days), :], turn, axis=1)[:, :columns].T

    direction, image = residual, operate(residual)
    now = inner(residual, residual)
    for step in range(ITERS - 1):
        alpha = now / inner(direction, image)
        factor = factor + alpha * direction
        residual = residual - alpha * image
        ahead, following = operate(residual), inner(residual, residual)
        beta = following / now
        direction = residual + beta * direction
        image = ahead + beta * image
        now = following
    alpha = now / inner(direction, image)
    results[0] = own(factor, 0) + alpha * own(direction, 1)
    results[1] = own(residual, 2) - alpha * own(image, 3)
    copies = []
    for i, target in enumerate((factor_hbm, residual_hbm)):
        copies.append(pltpu.make_async_copy(results.at[i], target, sems.at[i]))
        copies[i].start()
    for copy in copies:
        copy.wait()


def conjugate(coef, prev, mine, core, far, cross, gram, columns):
    days, width = prev.shape
    total = 2 * far.shape[0]
    shape = jax.ShapeDtypeStruct((columns, days), jnp.float32)
    return pl.pallas_call(
        functools.partial(cg_kernel, columns),
        compiler_params=pltpu.CompilerParams(vmem_limit_bytes=VMEM_BYTES),
        out_shape=(shape, shape),
        in_specs=[VMEM] * 7,
        out_specs=(HBM, HBM),
        scratch_shapes=[
            pltpu.VMEM((total, width), jnp.float32),
            pltpu.VMEM((total, width), jnp.float32),
            pltpu.VMEM((4, total, width), jnp.float32),
            pltpu.VMEM((2, columns, days), jnp.float32),
            pltpu.SemaphoreType.DMA((2,)),
        ],
        cost_estimate=pl.CostEstimate(
            flops=24 * total * width * width, bytes_accessed=4 * width * (width + 2 * total), transcendentals=0
        ),
    )(coef, prev, mine, core, far, cross, gram)


def bits_of(count):
    assert count & (count - 1) == 0 and count > 1
    return [1 << b for b in range(count.bit_length() - 1)]


def local(performance, student_factor, skill_factor, day_prev, ar_coef):
    days = performance.shape[0]
    half = days // 2
    rank = skill_factor.shape[1]
    stu_size, day_size = lax.axis_size("stu"), lax.axis_size("day")
    send, skill, perf, student = send_part(performance, student_factor, skill_factor)
    got = exchange(send, 1)
    keep, day_prev, coef = keep_part(perf, skill, student, day_prev, ar_coef)
    skill_gram = lax.dot_general(skill, skill, (((0,), (0,)), ((), ())), preferred_element_type=jnp.float32)
    payload = jnp.concatenate([keep[:half] + got, keep[half:]], 0)
    masks = [bit | 1 for bit in bits_of(stu_size)[:0:-1]]
    for mask, other in zip(masks, masks[:-2] + masks[:-3:-1], strict=True):
        got = exchange(payload, mask, other)
        if mask == masks[-1]:
            early = exchange(payload[half:], 1)
        if mask == masks[0]:
            got, skill_gram = lax.optimization_barrier((got, skill_gram))
        payload = jnp.concatenate([payload[:half] + got[:half], payload[half:], got[half:]], 0)
    mttkrp, students, late = payload[:half], payload[half:], got[half:]
    factor = lax.dynamic_slice_in_dim(day_prev, own_part() * half, half, 0)
    *bits, last = bits_of(day_size)
    for bit in bits:
        got = exchange(jnp.concatenate([mttkrp, factor], 0), bit * stu_size + 1)
        rows = bit * half
        mttkrp = jnp.concatenate([mttkrp, got[:rows]], 0)
        factor = jnp.concatenate([factor, got[rows:]], 0)
    mine = jnp.concatenate([mttkrp, factor[half:], late], 0)
    far = exchange(jnp.concatenate([mttkrp, factor], 0), last * stu_size + 1)
    core = exchange(mine, 1)
    stack = gram_stack(mine.shape[0] - late.shape[0], students, early, core, skill_gram)
    cross = exchange(far, 1)
    factor, residual = conjugate(coef, day_prev, mine, core, far, cross, stack, rank // stu_size)
    return factor.T, residual.T


def solution(mesh):
    return jax.shard_map(
        local,
        mesh=mesh,
        in_specs=(P("day", "stu", None), P("stu", None), P(), P("day", None), P()),
        out_specs=(P("day", "stu"), P("day", "stu")),
        check_vma=False,
    )
```

```python
import functools

import jax
import jax.numpy as jnp
from jax import lax
from jax.experimental import pallas as pl
from jax.experimental.pallas import tpu as pltpu
from jax.sharding import PartitionSpec as P

LAGS = 7
ITERS = 3
PAD = 8
LANES = 128
VMEM_BYTES = 8 << 20


smoothing = 1.0

VMEM = pl.BlockSpec(memory_space=pltpu.VMEM)
HBM = pl.BlockSpec(memory_space=pltpu.HBM)


def exchange(block, mask, other=None):
    both = mask, mask if other is None else other
    union = both[0] | both[1]
    route = [(i, i ^ both[(i & union).bit_count() % 2]) for i in range(lax.axis_size(("day", "stu")))]
    return lax.ppermute(block, ("day", "stu"), route)


def own_part():
    place = lax.axis_index("day") ^ lax.axis_index("stu")
    for shift in (8, 4, 2, 1):
        place = place ^ (place >> shift)
    return place & 1


def split(values):
    high = values.astype(jnp.bfloat16)
    return high, (values - high.astype(jnp.float32)).astype(jnp.bfloat16)


def product(a, b):
    return jnp.dot(a, b, preferred_element_type=jnp.float32)


def student_sums(perf, skill, wide, proj, out_ref):
    students = wide.shape[0]
    total = product(perf[...], skill[...])
    days = total.shape[0] // students
    for t in range(proj.shape[0]):
        lanes = slice(t * LANES, (t + 1) * LANES)
        proj[t, : total.shape[0], :] = total[:, lanes]
        terms = None
        for s in range(students):
            row = proj[t, pl.ds(s, days, stride=students), :] * wide[s : s + 1, lanes]
            terms = row if terms is None else terms + row
        out_ref[:days, lanes] = terms


def send_kernel(perf_hbm, skill_hbm, student_hbm, send_ref, skill, keep, student, perf, proj, sems):
    rows = perf.shape[0]
    part = own_part()
    away = perf_hbm.at[pl.ds(pl.multiple_of((1 - part) * rows, rows), rows)]
    home = perf_hbm.at[pl.ds(pl.multiple_of(part * rows, rows), rows)]
    copies = []
    for i, (source, target) in enumerate(
        ((student_hbm, student), (skill_hbm, skill), (away, perf), (home, keep))
    ):
        copies.append(pltpu.make_async_copy(source, target, sems.at[i]))
        copies[i].start()
    for copy in copies[:3]:
        copy.wait()
    student_sums(perf, skill, student[...].astype(jnp.float32), proj, send_ref)
    copies[3].wait()


def send_part(performance, student_factor, skill_factor):
    days, students, skills = performance.shape
    rank = skill_factor.shape[1]
    rows = days * students // 2
    operands = performance.reshape(2 * rows, skills), skill_factor, student_factor
    return pl.pallas_call(
        send_kernel,
        compiler_params=pltpu.CompilerParams(vmem_limit_bytes=VMEM_BYTES),
        out_shape=(
            jax.ShapeDtypeStruct((days // 2, rank), jnp.float32),
            jax.ShapeDtypeStruct((skills, rank), jnp.bfloat16),
            jax.ShapeDtypeStruct((rows, skills), jnp.bfloat16),
            jax.ShapeDtypeStruct((students, rank), jnp.bfloat16),
        ),
        in_specs=[HBM] * 3,
        out_specs=(VMEM,) * 4,
        scratch_shapes=[
            pltpu.VMEM((rows, skills), jnp.bfloat16),
            pltpu.VMEM((rank // LANES, rows + students, LANES), jnp.float32),
            pltpu.SemaphoreType.DMA((4,)),
        ],
        cost_estimate=pl.CostEstimate(
            flops=2 * rows * skills * rank, bytes_accessed=2 * (2 * rows + rank) * skills, transcendentals=0
        ),
    )(*(pltpu.with_memory_space_constraint(x, pltpu.HBM) for x in operands))


def keep_kernel(perf, skill, student, prev_hbm, coef_hbm, keep_ref, prev, coef, proj, sems):
    copies = [
        pltpu.make_async_copy(prev_hbm, prev, sems.at[0]),
        pltpu.make_async_copy(coef_hbm, coef, sems.at[1]),
    ]
    for copy in copies:
        copy.start()
    wide = student[...].astype(jnp.float32)
    student_sums(perf, skill, wide, proj, keep_ref)
    keep_ref[-wide.shape[0] :, :] = wide
    for copy in copies:
        copy.wait()


def keep_part(perf, skill, student, prev, coef):
    rows, skills = perf.shape
    students, rank = student.shape
    small = prev, coef.reshape(1, LAGS)
    return pl.pallas_call(
        keep_kernel,
        compiler_params=pltpu.CompilerParams(vmem_limit_bytes=VMEM_BYTES),
        out_shape=(
            jax.ShapeDtypeStruct((rows // students + students, rank), jnp.float32),
            *(jax.ShapeDtypeStruct(x.shape, x.dtype) for x in small),
        ),
        in_specs=[VMEM] * 3 + [HBM] * 2,
        out_specs=(VMEM,) * 3,
        scratch_shapes=[
            pltpu.VMEM((rank // LANES, rows + students, LANES), jnp.float32),
            pltpu.SemaphoreType.DMA((2,)),
        ],
        cost_estimate=pl.CostEstimate(
            flops=2 * rows * skills * rank, bytes_accessed=2 * (rows + rank) * skills, transcendentals=0
        ),
    )(perf, skill, student, *(pltpu.with_memory_space_constraint(x, pltpu.HBM) for x in small))


def gram_kernel(first, mine_ref, early_ref, late_ref, skill_gram_ref, out_ref):
    students = jnp.concatenate([mine_ref[...], early_ref[...], late_ref[first:, :]], 0).astype(jnp.bfloat16)
    student_gram = lax.dot_general(
        students, students, (((0,), (0,)), ((), ())), preferred_element_type=jnp.float32
    )
    rank = out_ref.shape[0]
    high, low = split(student_gram * skill_gram_ref[...])
    out_ref[:, :rank] = high
    out_ref[:, rank:] = low


def gram_stack(first, mine, early, late, skill_gram):
    count, rank = mine.shape
    return pl.pallas_call(
        functools.partial(gram_kernel, first),
        compiler_params=pltpu.CompilerParams(vmem_limit_bytes=VMEM_BYTES),
        out_shape=jax.ShapeDtypeStruct((rank, 2 * rank), jnp.bfloat16),
        in_specs=[VMEM] * 4,
        out_specs=VMEM,
        cost_estimate=pl.CostEstimate(
            flops=4 * count * rank * rank, bytes_accessed=8 * rank * rank, transcendentals=0
        ),
    )(mine, early, late, skill_gram)


def cg_kernel(
    columns, coef_ref, prev_ref, mine_ref, core_ref, far_ref, cross_ref, gram_ref, factor_hbm, residual_hbm,
    block, results, sems,
):
    days, width = prev_ref.shape
    total = 2 * far_ref.shape[0]
    near, half = total // days // 2, days // 2
    day, stu, part = lax.axis_index("day"), lax.axis_index("stu"), own_part()
    sums, starts = [], [prev_ref[...]]
    for b in range(2 * near):
        row, step = (b, near - 1) if b < near else (b - near, near)
        pair = (mine_ref, core_ref) if b < near else (far_ref, cross_ref)
        for into, at in ((sums, row), (starts, row + step)):
            if into is sums or b > 0:
                own, away = (source[at * half : (at + 1) * half, :] for source in pair)
                flip = part == 1
                into.append(jnp.concatenate([jnp.where(flip, away, own), jnp.where(flip, own, away)], 0))
    for k in range((2 * near).bit_length() - 1):
        flip = (day >> k) & 1 == 1
        sums, starts = (
            [jnp.where(flip, rows[d ^ (1 << k)], rows[d]) for d in range(2 * near)] for rows in (sums, starts)
        )
    mttkrp, values = jnp.concatenate(sums, 0), jnp.concatenate(starts, 0)
    gram_high, gram_wide = gram_ref[:, :width], gram_ref[...]
    blank = jnp.zeros((PAD, LANES), jnp.float32)
    coef = [coef_ref[:, l : l + 1] for l in range(LAGS)]

    def operate(v):
        v_high, v_low = split(v)
        both = product(jnp.concatenate([v_high, v_low], 0), gram_wide)
        mixed = both[:total, :width] + (both[total:, :width] + both[:total, width:])
        back = jnp.concatenate([smooth(v[:, t : t + LANES]) for t in range(0, width, LANES)], 1)
        return mixed + smoothing * back

    def smooth(v):
        padded = jnp.concatenate([blank, v], 0)
        ahead = v
        for lag in range(1, LAGS + 1):
            ahead = ahead - coef[lag - 1] * pltpu.roll(padded, lag, axis=0)[PAD:]
        padded = jnp.concatenate([ahead, blank], 0)
        back = ahead
        for lag in range(1, LAGS + 1):
            back = back - coef[lag - 1] * pltpu.roll(padded, total + PAD - lag, axis=0)[:total]
        return back

    def inner(a, b):
        terms = a * b
        tiles = [
            terms[i : i + PAD, j : j + LANES] for i in range(0, total, PAD) for j in range(0, width, LANES)
        ]
        while len(tiles) > 1:
            tiles = [x + y for x, y in zip(tiles[::2], tiles[1::2], strict=True)]
        return jnp.sum(jnp.sum(tiles[0], axis=1, keepdims=True), axis=0, keepdims=True)

    factor = values
    residual = mttkrp - operate(factor)
    start = pl.multiple_of(day * days, days)
    turn = jnp.where(stu == 0, 0, width - stu * columns)

    def own(v, slot):
        block[slot] = v
        return pltpu.roll(block[slot, pl.ds(start, days), :], turn, axis=1)[:, :columns].T

    direction, image = residual, operate(residual)
    now = inner(residual, residual)
    for step in range(ITERS - 1):
        alpha = now / inner(direction, image)
        factor = factor + alpha * direction
        residual = residual - alpha * image
        ahead, following = operate(residual), inner(residual, residual)
        beta = following / now
        direction = residual + beta * direction
        image = ahead + beta * image
        now = following
    alpha = now / inner(direction, image)
    results[0] = own(factor, 0) + alpha * own(direction, 1)
    results[1] = own(residual, 2) - alpha * own(image, 3)
    copies = []
    for i, target in enumerate((factor_hbm, residual_hbm)):
        copies.append(pltpu.make_async_copy(results.at[i], target, sems.at[i]))
        copies[i].start()
    for copy in copies:
        copy.wait()


def conjugate(coef, prev, mine, core, far, cross, gram, columns):
    days, width = prev.shape
    total = 2 * far.shape[0]
    shape = jax.ShapeDtypeStruct((columns, days), jnp.float32)
    return pl.pallas_call(
        functools.partial(cg_kernel, columns),
        compiler_params=pltpu.CompilerParams(vmem_limit_bytes=VMEM_BYTES),
        out_shape=(shape, shape),
        in_specs=[VMEM] * 7,
        out_specs=(HBM, HBM),
        scratch_shapes=[
            pltpu.VMEM((4, total, width), jnp.float32),
            pltpu.VMEM((2, columns, days), jnp.float32),
            pltpu.SemaphoreType.DMA((2,)),
        ],
        cost_estimate=pl.CostEstimate(
            flops=24 * total * width * width, bytes_accessed=4 * width * (width + 2 * total), transcendentals=0
        ),
    )(coef, prev, mine, core, far, cross, gram)


def bits_of(count):
    assert count & (count - 1) == 0 and count > 1
    return [1 << b for b in range(count.bit_length() - 1)]


def local(performance, student_factor, skill_factor, day_prev, ar_coef):
    days = performance.shape[0]
    half = days // 2
    rank = skill_factor.shape[1]
    stu_size, day_size = lax.axis_size("stu"), lax.axis_size("day")
    send, skill, perf, student = send_part(performance, student_factor, skill_factor)
    got = exchange(send, 1)
    keep, day_prev, coef = keep_part(perf, skill, student, day_prev, ar_coef)
    skill_gram = lax.dot_general(skill, skill, (((0,), (0,)), ((), ())), preferred_element_type=jnp.float32)
    payload = jnp.concatenate([keep[:half] + got, keep[half:]], 0)
    masks = [bit | 1 for bit in bits_of(stu_size)[:0:-1]]
    for mask, other in zip(masks, masks[:-2] + masks[:-3:-1], strict=True):
        got = exchange(payload, mask, other)
        if mask == masks[-1]:
            early = exchange(payload[half:], 1)
        if mask == masks[0]:
            got, skill_gram = lax.optimization_barrier((got, skill_gram))
        payload = jnp.concatenate([payload[:half] + got[:half], payload[half:], got[half:]], 0)
    mttkrp, students, late = payload[:half], payload[half:], got[half:]
    factor = lax.dynamic_slice_in_dim(day_prev, own_part() * half, half, 0)
    *bits, last = bits_of(day_size)
    for bit in bits:
        got = exchange(jnp.concatenate([mttkrp, factor], 0), bit * stu_size + 1)
        rows = bit * half
        mttkrp = jnp.concatenate([mttkrp, got[:rows]], 0)
        factor = jnp.concatenate([factor, got[rows:]], 0)
    mine = jnp.concatenate([mttkrp, factor[half:], late], 0)
    far = exchange(jnp.concatenate([mttkrp, factor], 0), last * stu_size + 1)
    core = exchange(mine, 1)
    stack = gram_stack(mine.shape[0] - late.shape[0], students, early, core, skill_gram)
    cross = exchange(far, 1)
    factor, residual = conjugate(coef, day_prev, mine, core, far, cross, stack, rank // stu_size)
    return factor.T, residual.T


def solution(mesh):
    return jax.shard_map(
        local,
        mesh=mesh,
        in_specs=(P("day", "stu", None), P("stu", None), P(), P("day", None), P()),
        out_specs=(P("day", "stu"), P("day", "stu")),
        check_vma=False,
    )
```

```python
import functools

import jax
import jax.numpy as jnp
from jax import lax
from jax.experimental import pallas as pl
from jax.experimental.pallas import tpu as pltpu
from jax.sharding import PartitionSpec as P

LAGS = 7
ITERS = 3
PAD = 8
LANES = 128
VMEM_BYTES = 8 << 20


smoothing = 1.0

VMEM = pl.BlockSpec(memory_space=pltpu.VMEM)
HBM = pl.BlockSpec(memory_space=pltpu.HBM)


def exchange(block, mask, other=None):
    both = mask, mask if other is None else other
    union = both[0] | both[1]
    route = [(i, i ^ both[(i & union).bit_count() % 2]) for i in range(lax.axis_size(("day", "stu")))]
    return lax.ppermute(block, ("day", "stu"), route)


def own_part():
    place = lax.axis_index("day") ^ lax.axis_index("stu")
    for shift in (8, 4, 2, 1):
        place = place ^ (place >> shift)
    return place & 1


def split(values):
    high = values.astype(jnp.bfloat16)
    return high, (values - high.astype(jnp.float32)).astype(jnp.bfloat16)


def product(a, b):
    return jnp.dot(a, b, preferred_element_type=jnp.float32)


def student_sums(perf, skill, wide, proj, out_ref):
    students = wide.shape[0]
    total = product(perf[...], skill[...])
    days = total.shape[0] // students
    for t in range(proj.shape[0]):
        lanes = slice(t * LANES, (t + 1) * LANES)
        proj[t, : total.shape[0], :] = total[:, lanes]
        terms = None
        for s in range(students):
            row = proj[t, pl.ds(s, days, stride=students), :] * wide[s : s + 1, lanes]
            terms = row if terms is None else terms + row
        out_ref[:days, lanes] = terms


def send_kernel(perf_hbm, skill_hbm, student_hbm, send_ref, skill, keep, student, perf, proj, sems):
    rows = perf.shape[0]
    part = own_part()
    away = perf_hbm.at[pl.ds(pl.multiple_of((1 - part) * rows, rows), rows)]
    home = perf_hbm.at[pl.ds(pl.multiple_of(part * rows, rows), rows)]
    copies = []
    for i, (source, target) in enumerate(
        ((student_hbm, student), (skill_hbm, skill), (away, perf), (home, keep))
    ):
        copies.append(pltpu.make_async_copy(source, target, sems.at[i]))
        copies[i].start()
    for copy in copies[:3]:
        copy.wait()
    student_sums(perf, skill, student[...].astype(jnp.float32), proj, send_ref)
    copies[3].wait()


def send_part(performance, student_factor, skill_factor):
    days, students, skills = performance.shape
    rank = skill_factor.shape[1]
    rows = days * students // 2
    operands = performance.reshape(2 * rows, skills), skill_factor, student_factor
    return pl.pallas_call(
        send_kernel,
        compiler_params=pltpu.CompilerParams(vmem_limit_bytes=VMEM_BYTES),
        out_shape=(
            jax.ShapeDtypeStruct((days // 2, rank), jnp.float32),
            jax.ShapeDtypeStruct((skills, rank), jnp.bfloat16),
            jax.ShapeDtypeStruct((rows, skills), jnp.bfloat16),
            jax.ShapeDtypeStruct((students, rank), jnp.bfloat16),
        ),
        in_specs=[HBM] * 3,
        out_specs=(VMEM,) * 4,
        scratch_shapes=[
            pltpu.VMEM((rows, skills), jnp.bfloat16),
            pltpu.VMEM((rank // LANES, rows + students, LANES), jnp.float32),
            pltpu.SemaphoreType.DMA((4,)),
        ],
        cost_estimate=pl.CostEstimate(
            flops=2 * rows * skills * rank, bytes_accessed=2 * (2 * rows + rank) * skills, transcendentals=0
        ),
    )(*(pltpu.with_memory_space_constraint(x, pltpu.HBM) for x in operands))


def keep_kernel(perf, skill, student, prev_hbm, coef_hbm, keep_ref, prev, coef, proj, sems):
    copies = [
        pltpu.make_async_copy(prev_hbm, prev, sems.at[0]),
        pltpu.make_async_copy(coef_hbm, coef, sems.at[1]),
    ]
    for copy in copies:
        copy.start()
    wide = student[...].astype(jnp.float32)
    student_sums(perf, skill, wide, proj, keep_ref)
    keep_ref[-wide.shape[0] :, :] = wide
    for copy in copies:
        copy.wait()


def keep_part(perf, skill, student, prev, coef):
    rows, skills = perf.shape
    students, rank = student.shape
    small = prev, coef.reshape(1, LAGS)
    return pl.pallas_call(
        keep_kernel,
        compiler_params=pltpu.CompilerParams(vmem_limit_bytes=VMEM_BYTES),
        out_shape=(
            jax.ShapeDtypeStruct((rows // students + students, rank), jnp.float32),
            *(jax.ShapeDtypeStruct(x.shape, x.dtype) for x in small),
        ),
        in_specs=[VMEM] * 3 + [HBM] * 2,
        out_specs=(VMEM,) * 3,
        scratch_shapes=[
            pltpu.VMEM((rank // LANES, rows + students, LANES), jnp.float32),
            pltpu.SemaphoreType.DMA((2,)),
        ],
        cost_estimate=pl.CostEstimate(
            flops=2 * rows * skills * rank, bytes_accessed=2 * (rows + rank) * skills, transcendentals=0
        ),
    )(perf, skill, student, *(pltpu.with_memory_space_constraint(x, pltpu.HBM) for x in small))


def gram_kernel(first, mine_ref, early_ref, late_ref, skill_gram_ref, out_ref):
    students = jnp.concatenate([mine_ref[...], early_ref[...], late_ref[first:, :]], 0).astype(jnp.bfloat16)
    student_gram = lax.dot_general(
        students, students, (((0,), (0,)), ((), ())), preferred_element_type=jnp.float32
    )
    rank = out_ref.shape[0]
    high, low = split(student_gram * skill_gram_ref[...])
    out_ref[:, :rank] = high
    out_ref[:, rank:] = low


def gram_stack(first, mine, early, late, skill_gram):
    count, rank = mine.shape
    return pl.pallas_call(
        functools.partial(gram_kernel, first),
        compiler_params=pltpu.CompilerParams(vmem_limit_bytes=VMEM_BYTES),
        out_shape=jax.ShapeDtypeStruct((rank, 2 * rank), jnp.bfloat16),
        in_specs=[VMEM] * 4,
        out_specs=VMEM,
        cost_estimate=pl.CostEstimate(
            flops=4 * count * rank * rank, bytes_accessed=8 * rank * rank, transcendentals=0
        ),
    )(mine, early, late, skill_gram)


def cg_kernel(
    columns, coef_ref, prev_ref, mine_ref, core_ref, far_ref, cross_ref, gram_ref, factor_hbm, residual_hbm,
    mttkrp, values, block, results, sems,
):
    days, width = prev_ref.shape
    total = mttkrp.shape[0]
    near, half = total // days // 2, days // 2
    day, stu, part = lax.axis_index("day"), lax.axis_index("stu"), own_part()
    values[pl.ds(pl.multiple_of(day * days, days), days), :] = prev_ref[...]
    for at, near_ref, away_ref in ((part, mine_ref, far_ref), (1 - part, core_ref, cross_ref)):
        for b in range(2 * near):
            source, row, step = (near_ref, b, near - 1) if b < near else (away_ref, b - near, near)
            place = pl.ds(pl.multiple_of((day ^ b) * days + at * half, half), half)
            mttkrp[place, :] = source[row * half : (row + 1) * half, :]
            if b > 0:
                values[place, :] = source[(row + step) * half : (row + step + 1) * half, :]
    gram_high, gram_wide = gram_ref[:, :width], gram_ref[...]
    blank = jnp.zeros((PAD, LANES), jnp.float32)
    coef = [coef_ref[:, l : l + 1] for l in range(LAGS)]

    def operate(v):
        v_high, v_low = split(v)
        both = product(jnp.concatenate([v_high, v_low], 0), gram_wide)
        mixed = both[:total, :width] + (both[total:, :width] + both[:total, width:])
        back = jnp.concatenate([smooth(v[:, t : t + LANES]) for t in range(0, width, LANES)], 1)
        return mixed + smoothing * back

    def smooth(v):
        padded = jnp.concatenate([blank, v], 0)
        ahead = v
        for lag in range(1, LAGS + 1):
            ahead = ahead - coef[lag - 1] * pltpu.roll(padded, lag, axis=0)[PAD:]
        padded = jnp.concatenate([ahead, blank], 0)
        back = ahead
        for lag in range(1, LAGS + 1):
            back = back - coef[lag - 1] * pltpu.roll(padded, total + PAD - lag, axis=0)[:total]
        return back

    def inner(a, b):
        terms = a * b
        tiles = [
            terms[i : i + PAD, j : j + LANES] for i in range(0, total, PAD) for j in range(0, width, LANES)
        ]
        while len(tiles) > 1:
            tiles = [x + y for x, y in zip(tiles[::2], tiles[1::2], strict=True)]
        return jnp.sum(jnp.sum(tiles[0], axis=1, keepdims=True), axis=0, keepdims=True)

    factor = values[...]
    residual = mttkrp[...] - operate(factor)
    start = pl.multiple_of(day * days, days)
    turn = jnp.where(stu == 0, 0, width - stu * columns)

    def own(v, slot):
        block[slot] = v
        return pltpu.roll(block[slot, pl.ds(start, days), :], turn, axis=1)[:, :columns].T

    direction, image = residual, operate(residual)
    now = inner(residual, residual)
    for step in range(ITERS - 1):
        alpha = now / inner(direction, image)
        factor = factor + alpha * direction
        residual = residual - alpha * image
        ahead, following = operate(residual), inner(residual, residual)
        beta = following / now
        direction = residual + beta * direction
        image = ahead + beta * image
        now = following
    alpha = now / inner(direction, image)
    results[0] = own(factor, 0) + alpha * own(direction, 1)
    results[1] = own(residual, 2) - alpha * own(image, 3)
    copies = []
    for i, target in enumerate((factor_hbm, residual_hbm)):
        copies.append(pltpu.make_async_copy(results.at[i], target, sems.at[i]))
        copies[i].start()
    for copy in copies:
        copy.wait()


def conjugate(coef, prev, mine, core, far, cross, gram, columns):
    days, width = prev.shape
    total = 2 * far.shape[0]
    shape = jax.ShapeDtypeStruct((columns, days), jnp.float32)
    return pl.pallas_call(
        functools.partial(cg_kernel, columns),
        compiler_params=pltpu.CompilerParams(vmem_limit_bytes=VMEM_BYTES),
        out_shape=(shape, shape),
        in_specs=[VMEM] * 7,
        out_specs=(HBM, HBM),
        scratch_shapes=[
            pltpu.VMEM((total, width), jnp.float32),
            pltpu.VMEM((total, width), jnp.float32),
            pltpu.VMEM((4, total, width), jnp.float32),
            pltpu.VMEM((2, columns, days), jnp.float32),
            pltpu.SemaphoreType.DMA((2,)),
        ],
        cost_estimate=pl.CostEstimate(
            flops=24 * total * width * width, bytes_accessed=4 * width * (width + 2 * total), transcendentals=0
        ),
    )(coef, prev, mine, core, far, cross, gram)


def bits_of(count):
    assert count & (count - 1) == 0 and count > 1
    return [1 << b for b in range(count.bit_length() - 1)]


def local(performance, student_factor, skill_factor, day_prev, ar_coef):
    days = performance.shape[0]
    half = days // 2
    rank = skill_factor.shape[1]
    stu_size, day_size = lax.axis_size("stu"), lax.axis_size("day")
    send, skill, perf, student = send_part(performance, student_factor, skill_factor)
    got = exchange(send, 1)
    keep, day_prev, coef = keep_part(perf, skill, student, day_prev, ar_coef)
    skill_gram = lax.dot_general(skill, skill, (((0,), (0,)), ((), ())), preferred_element_type=jnp.float32)
    payload = jnp.concatenate([keep[:half] + got, keep[half:]], 0)
    masks = [bit | 1 for bit in bits_of(stu_size)[:0:-1]]
    for mask, other in zip(masks, masks[:-2] + masks[:-3:-1], strict=True):
        got = exchange(payload, mask, other)
        if mask == masks[-1]:
            early = exchange(payload[half:], 1)
        if mask == masks[0]:
            got, skill_gram = lax.optimization_barrier((got, skill_gram))
        payload = jnp.concatenate([payload[:half] + got[:half], payload[half:], got[half:]], 0)
    mttkrp, students, late = payload[:half], payload[half:], got[half:]
    factor = lax.dynamic_slice_in_dim(day_prev, own_part() * half, half, 0)
    *bits, last = bits_of(day_size)
    for bit in bits:
        got = exchange(jnp.concatenate([mttkrp, factor], 0), bit * stu_size + 1)
        rows = bit * half
        mttkrp = jnp.concatenate([mttkrp, got[:rows]], 0)
        factor = jnp.concatenate([factor, got[rows:]], 0)
    mine = jnp.concatenate([mttkrp, factor[half:], late], 0)
    far = exchange(jnp.concatenate([mttkrp, factor], 0), last * stu_size + 1)
    core = exchange(mine, 1)
    stack = gram_stack(mine.shape[0] - late.shape[0], students, early, core, skill_gram)
    far, stack = lax.optimization_barrier((far, stack))
    cross = exchange(far, 1)
    factor, residual = conjugate(coef, day_prev, mine, core, far, cross, stack, rank // stu_size)
    return factor.T, residual.T


def solution(mesh):
    return jax.shard_map(
        local,
        mesh=mesh,
        in_specs=(P("day", "stu", None), P("stu", None), P(), P("day", None), P()),
        out_specs=(P("day", "stu"), P("day", "stu")),
        check_vma=False,
    )
```

```python
import functools

import jax
import jax.numpy as jnp
from jax import lax
from jax.experimental import pallas as pl
from jax.experimental.pallas import tpu as pltpu
from jax.sharding import PartitionSpec as P

LAGS = 7
ITERS = 3
PAD = 8
LANES = 128
VMEM_BYTES = 8 << 20


smoothing = 1.0

VMEM = pl.BlockSpec(memory_space=pltpu.VMEM)
HBM = pl.BlockSpec(memory_space=pltpu.HBM)


def exchange(block, mask, other=None):
    both = mask, mask if other is None else other
    union = both[0] | both[1]
    route = [(i, i ^ both[(i & union).bit_count() % 2]) for i in range(lax.axis_size(("day", "stu")))]
    return lax.ppermute(block, ("day", "stu"), route)


def own_part():
    place = lax.axis_index("day") ^ lax.axis_index("stu")
    for shift in (8, 4, 2, 1):
        place = place ^ (place >> shift)
    return place & 1


def split(values):
    high = values.astype(jnp.bfloat16)
    return high, (values - high.astype(jnp.float32)).astype(jnp.bfloat16)


def product(a, b):
    return jnp.dot(a, b, preferred_element_type=jnp.float32)


def student_sums(perf, skill, wide, proj, out_ref):
    students = wide.shape[0]
    depth = perf.shape[1] // 2
    total = product(perf[:, :depth], skill[:depth, :]) + product(perf[:, depth:], skill[depth:, :])
    days = total.shape[0] // students
    for t in range(proj.shape[0]):
        lanes = slice(t * LANES, (t + 1) * LANES)
        proj[t, : total.shape[0], :] = total[:, lanes]
        terms = None
        for s in range(students):
            row = proj[t, pl.ds(s, days, stride=students), :] * wide[s : s + 1, lanes]
            terms = row if terms is None else terms + row
        out_ref[:days, lanes] = terms


def send_kernel(perf_hbm, skill_hbm, student_hbm, send_ref, skill, keep, student, perf, proj, sems):
    rows = perf.shape[0]
    part = own_part()
    away = perf_hbm.at[pl.ds(pl.multiple_of((1 - part) * rows, rows), rows)]
    home = perf_hbm.at[pl.ds(pl.multiple_of(part * rows, rows), rows)]
    copies = []
    for i, (source, target) in enumerate(
        ((student_hbm, student), (skill_hbm, skill), (away, perf), (home, keep))
    ):
        copies.append(pltpu.make_async_copy(source, target, sems.at[i]))
        copies[i].start()
    for copy in copies[:3]:
        copy.wait()
    student_sums(perf, skill, student[...].astype(jnp.float32), proj, send_ref)
    copies[3].wait()


def send_part(performance, student_factor, skill_factor):
    days, students, skills = performance.shape
    rank = skill_factor.shape[1]
    rows = days * students // 2
    operands = performance.reshape(2 * rows, skills), skill_factor, student_factor
    return pl.pallas_call(
        send_kernel,
        compiler_params=pltpu.CompilerParams(vmem_limit_bytes=VMEM_BYTES),
        out_shape=(
            jax.ShapeDtypeStruct((days // 2, rank), jnp.float32),
            jax.ShapeDtypeStruct((skills, rank), jnp.bfloat16),
            jax.ShapeDtypeStruct((rows, skills), jnp.bfloat16),
            jax.ShapeDtypeStruct((students, rank), jnp.bfloat16),
        ),
        in_specs=[HBM] * 3,
        out_specs=(VMEM,) * 4,
        scratch_shapes=[
            pltpu.VMEM((rows, skills), jnp.bfloat16),
            pltpu.VMEM((rank // LANES, rows + students, LANES), jnp.float32),
            pltpu.SemaphoreType.DMA((4,)),
        ],
        cost_estimate=pl.CostEstimate(
            flops=2 * rows * skills * rank, bytes_accessed=2 * (2 * rows + rank) * skills, transcendentals=0
        ),
    )(*(pltpu.with_memory_space_constraint(x, pltpu.HBM) for x in operands))


def keep_kernel(perf, skill, student, prev_hbm, coef_hbm, keep_ref, prev, coef, proj, sems):
    copies = [
        pltpu.make_async_copy(prev_hbm, prev, sems.at[0]),
        pltpu.make_async_copy(coef_hbm, coef, sems.at[1]),
    ]
    for copy in copies:
        copy.start()
    wide = student[...].astype(jnp.float32)
    student_sums(perf, skill, wide, proj, keep_ref)
    keep_ref[-wide.shape[0] :, :] = wide
    for copy in copies:
        copy.wait()


def keep_part(perf, skill, student, prev, coef):
    rows, skills = perf.shape
    students, rank = student.shape
    small = prev, coef.reshape(1, LAGS)
    return pl.pallas_call(
        keep_kernel,
        compiler_params=pltpu.CompilerParams(vmem_limit_bytes=VMEM_BYTES),
        out_shape=(
            jax.ShapeDtypeStruct((rows // students + students, rank), jnp.float32),
            *(jax.ShapeDtypeStruct(x.shape, x.dtype) for x in small),
        ),
        in_specs=[VMEM] * 3 + [HBM] * 2,
        out_specs=(VMEM,) * 3,
        scratch_shapes=[
            pltpu.VMEM((rank // LANES, rows + students, LANES), jnp.float32),
            pltpu.SemaphoreType.DMA((2,)),
        ],
        cost_estimate=pl.CostEstimate(
            flops=2 * rows * skills * rank, bytes_accessed=2 * (rows + rank) * skills, transcendentals=0
        ),
    )(perf, skill, student, *(pltpu.with_memory_space_constraint(x, pltpu.HBM) for x in small))


def gram_kernel(first, mine_ref, early_ref, late_ref, skill_gram_ref, out_ref):
    students = jnp.concatenate([mine_ref[...], early_ref[...], late_ref[first:, :]], 0).astype(jnp.bfloat16)
    student_gram = lax.dot_general(
        students, students, (((0,), (0,)), ((), ())), preferred_element_type=jnp.float32
    )
    rank = out_ref.shape[0]
    high, low = split(student_gram * skill_gram_ref[...])
    out_ref[:, :rank] = high
    out_ref[:, rank:] = low


def gram_stack(first, mine, early, late, skill_gram):
    count, rank = mine.shape
    return pl.pallas_call(
        functools.partial(gram_kernel, first),
        compiler_params=pltpu.CompilerParams(vmem_limit_bytes=VMEM_BYTES),
        out_shape=jax.ShapeDtypeStruct((rank, 2 * rank), jnp.bfloat16),
        in_specs=[VMEM] * 4,
        out_specs=VMEM,
        cost_estimate=pl.CostEstimate(
            flops=4 * count * rank * rank, bytes_accessed=8 * rank * rank, transcendentals=0
        ),
    )(mine, early, late, skill_gram)


def cg_kernel(
    columns, coef_ref, prev_ref, mine_ref, core_ref, far_ref, cross_ref, gram_ref, factor_hbm, residual_hbm,
    mttkrp, values, block, results, sems,
):
    days, width = prev_ref.shape
    total = mttkrp.shape[0]
    near, half = total // days // 2, days // 2
    day, stu, part = lax.axis_index("day"), lax.axis_index("stu"), own_part()
    values[pl.ds(pl.multiple_of(day * days, days), days), :] = prev_ref[...]
    for at, near_ref, away_ref in ((part, mine_ref, far_ref), (1 - part, core_ref, cross_ref)):
        for b in range(2 * near):
            source, row, step = (near_ref, b, near - 1) if b < near else (away_ref, b - near, near)
            place = pl.ds(pl.multiple_of((day ^ b) * days + at * half, half), half)
            mttkrp[place, :] = source[row * half : (row + 1) * half, :]
            if b > 0:
                values[place, :] = source[(row + step) * half : (row + step + 1) * half, :]
    gram_high, gram_wide = gram_ref[:, :width], gram_ref[...]
    blank = jnp.zeros((PAD, LANES), jnp.float32)
    coef = [coef_ref[:, l : l + 1] for l in range(LAGS)]

    def operate(v):
        v_high, v_low = split(v)
        both = product(jnp.concatenate([v_high, v_low], 0), gram_wide)
        mixed = both[:total, :width] + (both[total:, :width] + both[:total, width:])
        back = jnp.concatenate([smooth(v[:, t : t + LANES]) for t in range(0, width, LANES)], 1)
        return mixed + smoothing * back

    def smooth(v):
        padded = jnp.concatenate([blank, v], 0)
        ahead = v
        for lag in range(1, LAGS + 1):
            ahead = ahead - coef[lag - 1] * pltpu.roll(padded, lag, axis=0)[PAD:]
        padded = jnp.concatenate([ahead, blank], 0)
        back = ahead
        for lag in range(1, LAGS + 1):
            back = back - coef[lag - 1] * pltpu.roll(padded, total + PAD - lag, axis=0)[:total]
        return back

    def inner(a, b):
        terms = a * b
        tiles = [
            terms[i : i + PAD, j : j + LANES] for i in range(0, total, PAD) for j in range(0, width, LANES)
        ]
        while len(tiles) > 1:
            tiles = [x + y for x, y in zip(tiles[::2], tiles[1::2], strict=True)]
        return jnp.sum(jnp.sum(tiles[0], axis=1, keepdims=True), axis=0, keepdims=True)

    factor = values[...]
    residual = mttkrp[...] - operate(factor)
    start = pl.multiple_of(day * days, days)
    turn = jnp.where(stu == 0, 0, width - stu * columns)

    def own(v, slot):
        block[slot] = v
        return pltpu.roll(block[slot, pl.ds(start, days), :], turn, axis=1)[:, :columns].T

    direction, image = residual, operate(residual)
    now = inner(residual, residual)
    for step in range(ITERS - 1):
        alpha = now / inner(direction, image)
        factor = factor + alpha * direction
        residual = residual - alpha * image
        ahead, following = operate(residual), inner(residual, residual)
        beta = following / now
        direction = residual + beta * direction
        image = ahead + beta * image
        now = following
    alpha = now / inner(direction, image)
    results[0] = own(factor, 0) + alpha * own(direction, 1)
    results[1] = own(residual, 2) - alpha * own(image, 3)
    copies = []
    for i, target in enumerate((factor_hbm, residual_hbm)):
        copies.append(pltpu.make_async_copy(results.at[i], target, sems.at[i]))
        copies[i].start()
    for copy in copies:
        copy.wait()


def conjugate(coef, prev, mine, core, far, cross, gram, columns):
    days, width = prev.shape
    total = 2 * far.shape[0]
    shape = jax.ShapeDtypeStruct((columns, days), jnp.float32)
    return pl.pallas_call(
        functools.partial(cg_kernel, columns),
        compiler_params=pltpu.CompilerParams(vmem_limit_bytes=VMEM_BYTES),
        out_shape=(shape, shape),
        in_specs=[VMEM] * 7,
        out_specs=(HBM, HBM),
        scratch_shapes=[
            pltpu.VMEM((total, width), jnp.float32),
            pltpu.VMEM((total, width), jnp.float32),
            pltpu.VMEM((4, total, width), jnp.float32),
            pltpu.VMEM((2, columns, days), jnp.float32),
            pltpu.SemaphoreType.DMA((2,)),
        ],
        cost_estimate=pl.CostEstimate(
            flops=24 * total * width * width, bytes_accessed=4 * width * (width + 2 * total), transcendentals=0
        ),
    )(coef, prev, mine, core, far, cross, gram)


def bits_of(count):
    assert count & (count - 1) == 0 and count > 1
    return [1 << b for b in range(count.bit_length() - 1)]


def local(performance, student_factor, skill_factor, day_prev, ar_coef):
    days = performance.shape[0]
    half = days // 2
    rank = skill_factor.shape[1]
    stu_size, day_size = lax.axis_size("stu"), lax.axis_size("day")
    send, skill, perf, student = send_part(performance, student_factor, skill_factor)
    got = exchange(send, 1)
    keep, day_prev, coef = keep_part(perf, skill, student, day_prev, ar_coef)
    skill_gram = lax.dot_general(skill, skill, (((0,), (0,)), ((), ())), preferred_element_type=jnp.float32)
    payload = jnp.concatenate([keep[:half] + got, keep[half:]], 0)
    masks = [bit | 1 for bit in bits_of(stu_size)[:0:-1]]
    for mask, other in zip(masks, masks[:-2] + masks[:-3:-1], strict=True):
        got = exchange(payload, mask, other)
        if mask == masks[-1]:
            early = exchange(payload[half:], 1)
        if mask == masks[0]:
            got, skill_gram = lax.optimization_barrier((got, skill_gram))
        payload = jnp.concatenate([payload[:half] + got[:half], payload[half:], got[half:]], 0)
    mttkrp, students, late = payload[:half], payload[half:], got[half:]
    factor = lax.dynamic_slice_in_dim(day_prev, own_part() * half, half, 0)
    *bits, last = bits_of(day_size)
    for bit in bits:
        got = exchange(jnp.concatenate([mttkrp, factor], 0), bit * stu_size + 1)
        rows = bit * half
        mttkrp = jnp.concatenate([mttkrp, got[:rows]], 0)
        factor = jnp.concatenate([factor, got[rows:]], 0)
    mine = jnp.concatenate([mttkrp, factor[half:], late], 0)
    far = exchange(jnp.concatenate([mttkrp, factor], 0), last * stu_size + 1)
    core = exchange(mine, 1)
    stack = gram_stack(mine.shape[0] - late.shape[0], students, early, core, skill_gram)
    cross = exchange(far, 1)
    factor, residual = conjugate(coef, day_prev, mine, core, far, cross, stack, rank // stu_size)
    return factor.T, residual.T


def solution(mesh):
    return jax.shard_map(
        local,
        mesh=mesh,
        in_specs=(P("day", "stu", None), P("stu", None), P(), P("day", None), P()),
        out_specs=(P("day", "stu"), P("day", "stu")),
        check_vma=False,
    )
```
